32 devices in a mesh: req: 4 (over z), head: 2 (over core), exp: 4 (over y, x).
Axes of the slice: x: 2, y: 2, z: 4, core: 2. Of those that a mesh axis runs over, the one named last changes fastest.
Arguments:
- queries: bfloat16 [64, 64, 128], P(('req', 'exp'), 'head'), may hold values from -18 to 18
- keys: bfloat16 [64, 512, 4, 128], P(('req', 'exp'), None, 'head'), may hold values from -15 to 15
- values: bfloat16 [64, 512, 4, 128], P(('req', 'exp'), None, 'head'), may hold values from -12 to 12
- lengths: int32 [64], P(('req', 'exp')), may hold values from 1 to 512, as said below
- out_weight: bfloat16 [8192, 4096], P('head', 'exp'), may hold values from -0.0625 to 0.0625
- resid: bfloat16 [64, 4096], P('req', 'exp'), may hold values from -11 to 11
- norm_gain: float32 [4096], replicated, may hold values from 0.25 to 1.75
- expert_ids: int32 [64, 8], P('req'), may hold values from 0 to 15, all different within a row; in each aligned block of 16 rows (0 to 15, 16 to 31, ...) at most 8 rows name the same one
- route_weights: float32 [64, 8], P('req'), may hold values from 0.1 to 1
- w_gate: bfloat16 [16, 4096, 768], P(('req', 'exp'), None, 'head'), may hold values from -0.09375 to 0.09375
- w_up: bfloat16 [16, 4096, 768], P(('req', 'exp'), None, 'head'), may hold values from -0.09375 to 0.09375
- w_down: bfloat16 [16, 768, 4096], P(('req', 'exp'), 'head'), may hold values from -0.21875 to 0.21875
Outputs:
- layer_out: bfloat16 [64, 4096], P('req', 'exp')
The draws below stay inside these ranges and needn't reach their ends.
Inputs may be any that keep to these rules, and one draw needn't show every extreme that they name: `expert_ids`: within each aligned block of 16 rows (the tokens of one index of req), a row names 8 different experts and no expert is named by more than 8 rows; some expert is named by exactly 8 rows. `lengths`: some question's cache is full.
All inputs are finite; a program needn't handle non-finite values.
Results may differ from the reference program's by a relative error of at most 0.0049.
Values may be sent and summed in bfloat16 or wider, within the bound.
No kernel may reach another device: no remote copies, remote signals or barrier semaphores. Data moves between devices by JAX's collectives and lax.ppermute only.
A program may use at most 64 MiB of HBM per device.

```python
import math
import jax
import jax.numpy as jnp
import numpy as np
from jax import lax

D = 4096
QUERY_HEADS = 64
KEY_VALUE_HEADS = 4
HEAD_DIMENSION = 128
FFE = 768
TOPK = 8
CONTEXT_SLOTS = 512
CAP = 8
GROUP = 16
TOKEN_COUNT = 64
EXPERTS = 16
N_REQ = 4


def draw_queries(key, part):
    return jnp.clip(jax.random.normal(key, (TOKEN_COUNT, QUERY_HEADS, HEAD_DIMENSION), jnp.float32), -6.0, 6.0).astype(jnp.bfloat16)


def draw_keys(key, part):
    return jnp.clip(jax.random.normal(key, (TOKEN_COUNT, CONTEXT_SLOTS, KEY_VALUE_HEADS, HEAD_DIMENSION), jnp.float32), -6.0, 6.0).astype(jnp.bfloat16)


def draw_lengths(key, part):
    leading_key, second_key = jax.random.split(key)
    shifts = jax.random.randint(leading_key, (TOKEN_COUNT,), 0, 4)
    jitter = jax.random.randint(second_key, (TOKEN_COUNT,), 0, CONTEXT_SLOTS // 16)
    result = jnp.right_shift(jnp.full((TOKEN_COUNT,), CONTEXT_SLOTS, jnp.int32), shifts.astype(jnp.int32)) - jitter.astype(jnp.int32)
    return result.at[0].set(CONTEXT_SLOTS).astype(jnp.int32)


def draw_resid(key, part):
    columns = jnp.arange(D, dtype=jnp.float32) / (D - 1)
    scales = jnp.exp(math.log(0.6) + math.log(3.0) * columns)
    return (jnp.clip(jax.random.normal(key, (TOKEN_COUNT, D), jnp.float32), -6.0, 6.0) * scales[None, :]).astype(jnp.bfloat16)


def level_of(key, dims, pieces, least, high):
    def one(dim, blocks):
        heights = jax.random.uniform(jax.random.fold_in(jax.random.fold_in(key, 6), dim), (blocks,), jnp.float32, least / len(pieces), high / len(pieces))
        return jnp.repeat(jnp.exp(heights), dims[dim] // blocks).reshape((-1,) + (1,) * (len(dims) - dim - 1))

    gain = one(*pieces[0])
    for cut in pieces[1:]:
        gain = gain * one(*cut)
    return gain


def assign_block(rng, own, number, rows, count, top, bound, slope):
    ranking = jax.random.permutation(rng, count)
    packed, common = load_shares(count, rows * top, bound, slope, True), load_shares(count, rows * top, bound, slope, False)
    places = jnp.arange(count)

    def named(tallies, turn):
        used = int((tallies > 0).sum())
        fixed = max(1, used // 4)
        passed = fixed + (places - fixed + turn * (used - fixed)) % max(1, count - fixed)
        return jnp.zeros((count,), jnp.int32).at[ranking[jnp.where(places < fixed, places, passed)]].set(jnp.asarray(tallies, jnp.int32))

    tallies = jnp.where(number % 4 == 0, named(packed, number // 4), named(common, number - number // 4 - 1))
    mixed = jax.random.permutation(jax.random.fold_in(own, 3), count)
    giver, sink = mixed[0:count // 2 * 2:2], mixed[1:count // 2 * 2:2]
    slack = jnp.minimum(tallies[giver] - 1, bound - tallies[sink]) // 2
    slack = jnp.where((giver == ranking[0]) | (sink == ranking[0]) | (tallies[sink] == 0), 0, jnp.maximum(slack, 0))
    passed = jax.random.randint(jax.random.fold_in(own, 4), (count // 2,), 0, 1 << 20) % (slack + 1)
    tallies = tallies.at[giver].add(-passed).at[sink].add(passed)
    members = jnp.searchsorted(jnp.cumsum(tallies), jnp.arange(rows * top), side="right").astype(jnp.int32)
    listing = members.reshape(top, rows).T
    listing = listing[jax.random.permutation(jax.random.fold_in(own, 1), rows)]
    turn = jax.random.randint(jax.random.fold_in(own, 2), (rows, 1), 0, top)
    return jnp.take_along_axis(listing, (jnp.arange(top)[None, :] + turn) % top, axis=1)


def load_shares(count, total, limit, lean, full):
    weights = [(1 << 20) // math.isqrt(grade ** lean) + 1 for grade in range(1, count + 1)]
    largest = limit if full else min(limit, max(-(-total // count), total * weights[0] // sum(weights)))
    least = 1 if total - largest >= count - 1 else 0
    counts, surplus = [largest] + [least] * (count - 1), total - largest - least * (count - 1)
    while surplus > 0:
        movable = [i for i in range(1, count) if counts[i] < largest] or [i for i in range(1, count) if counts[i] < limit]
        pool, budget = sum([weights[i] for i in movable]), surplus
        for i in movable:
            more = min(limit - counts[i], max(1, budget * weights[i] // pool), surplus)
            counts[i] = counts[i] + more
            surplus = surplus - more
    return np.array(counts)


def gaussian(stream_key, dims, scale, limit, cuts=(), held_as=jnp.bfloat16):
    entries = scale * jax.random.normal(stream_key, dims, jnp.float32)
    if cuts:
        entries = entries * level_of(stream_key, dims, cuts, -0.22, 0.18)
    return jnp.clip(entries, -limit, limit).astype(held_as)


def setup_inputs(seed: int = 0) -> dict:
    key_list = jax.random.split(jax.random.key(seed), 13)
    queries = draw_queries(jax.random.fold_in(key_list[12], 71), 0)
    keys = draw_keys(jax.random.fold_in(key_list[12], 71), 0)
    values = gaussian(key_list[2], (TOKEN_COUNT, CONTEXT_SLOTS, KEY_VALUE_HEADS, HEAD_DIMENSION), 2.0, 12.0, ((0, 16), (2, 2)))
    lengths = draw_lengths(jax.random.fold_in(key_list[12], 71), 0)
    out_weight = gaussian(key_list[4], (QUERY_HEADS * HEAD_DIMENSION, D), (QUERY_HEADS * HEAD_DIMENSION) ** -0.5, 0.0625, ((0, 2), (1, 4)))
    resid = draw_resid(jax.random.fold_in(key_list[12], 71), 0)
    norm_gain = jnp.clip(1.0 + 0.15 * jax.random.normal(key_list[6], (D,), jnp.float32), 0.25, 1.75)
    expert_ids_keys = jax.random.split(jax.random.fold_in(key_list[7], 1), TOKEN_COUNT // GROUP)
    expert_ids_turns = jax.random.permutation(jax.random.fold_in(key_list[7], 3), TOKEN_COUNT // GROUP)
    expert_ids = jax.vmap(lambda own, number: assign_block(jax.random.fold_in(key_list[7], 2), own, number, GROUP, EXPERTS, TOPK, CAP, 1))(expert_ids_keys, expert_ids_turns).reshape((TOKEN_COUNT, TOPK))
    route_weights = jnp.clip(jnp.exp(math.log(1.0) - 2.3025851 * jax.random.uniform(key_list[8], (TOKEN_COUNT, TOPK), jnp.float32) ** level_of(key_list[8], (TOKEN_COUNT, TOPK), ((0, 4),), -0.2, 0.2)), 0.1, 1.0)
    w_gate = gaussian(key_list[9], (EXPERTS, D, FFE), D ** -0.5, 0.09375, ((0, 16), (2, 2)))
    w_up = gaussian(key_list[10], (EXPERTS, D, FFE), D ** -0.5, 0.09375, ((0, 16), (2, 2)))
    w_down = gaussian(key_list[11], (EXPERTS, FFE, D), FFE ** -0.5, 0.21875, ((0, 16), (1, 2)))
    return dict(queries=queries, keys=keys, values=values, lengths=lengths, out_weight=out_weight, resid=resid, norm_gain=norm_gain, expert_ids=expert_ids, route_weights=route_weights, w_gate=w_gate, w_up=w_up, w_down=w_down)


def attend_token(operands):
    query_vector, key_rows, value_rows, length = operands
    grouped_result = query_vector.astype(jnp.float32).reshape(KEY_VALUE_HEADS, QUERY_HEADS // KEY_VALUE_HEADS, HEAD_DIMENSION)
    logits = jnp.einsum('gjd,cgd->gjc', grouped_result, key_rows.astype(jnp.float32)) * (1.0 / math.sqrt(HEAD_DIMENSION))
    visible = jnp.arange(CONTEXT_SLOTS, dtype=jnp.int32) < length
    logits = jnp.where(visible[None, None, :], logits, -1e+30)
    peak = lax.optimization_barrier(jnp.max(logits, axis=-1, keepdims=True))
    raised = jnp.exp(logits - peak)
    soft_weights = (raised / lax.optimization_barrier(jnp.sum(raised, axis=-1, keepdims=True))).astype(jnp.bfloat16)
    mixed = jnp.einsum('gjc,cgd->gjd', soft_weights.astype(jnp.float32), value_rows.astype(jnp.float32))
    return mixed.reshape(QUERY_HEADS * HEAD_DIMENSION).astype(jnp.bfloat16)

def reference(queries, keys, values, lengths, out_weight, resid, norm_gain, expert_ids, route_weights, w_gate, w_up, w_down):
    attended = lax.map(attend_token, (queries, keys, values, lengths))
    hidden = resid.astype(jnp.float32) + jnp.dot(attended, out_weight, preferred_element_type=jnp.float32)
    meansq = lax.optimization_barrier(jnp.mean(hidden * hidden, axis=1, keepdims=True))
    normed = (hidden * lax.rsqrt(meansq + 1e-06) * norm_gain).astype(jnp.bfloat16)
    slot_total = N_REQ * CAP

    def per_expert(total, operands):
        expert, gate_w, up_w, down_w = operands
        matched = expert_ids == expert
        chosen = jnp.any(matched, axis=1)
        weighting = lax.optimization_barrier(jnp.sum(jnp.where(matched, route_weights, 0.0), axis=1))
        position = jnp.cumsum(chosen.astype(jnp.int32)) - 1
        selector = (position[None, :] == jnp.arange(slot_total, dtype=jnp.int32)[:, None]) & chosen[None, :]
        rows = jnp.dot(selector.astype(jnp.bfloat16), normed, preferred_element_type=jnp.float32).astype(jnp.bfloat16)
        gate_act = jnp.dot(rows, gate_w, preferred_element_type=jnp.float32)
        up_act = jnp.dot(rows, up_w, preferred_element_type=jnp.float32)
        activated = (jax.nn.silu(gate_act) * up_act).astype(jnp.bfloat16)
        expert_out = jnp.dot(activated, down_w, preferred_element_type=jnp.float32)
        spread = jnp.where(selector, weighting[None, :], 0.0)
        return (total + jnp.dot(spread.T, expert_out, precision=lax.Precision.HIGHEST), None)
    start_total = jnp.zeros((TOKEN_COUNT, D), jnp.float32)
    mixture, _ = lax.scan(per_expert, start_total, (jnp.arange(EXPERTS, dtype=jnp.int32), w_gate, w_up, w_down))
    return (hidden + mixture).astype(jnp.bfloat16)
```

```python
import functools
import math

import jax
import jax.numpy as jnp
from jax import lax
from jax.experimental import pallas as pl
from jax.experimental.pallas import tpu as pltpu
from jax.sharding import PartitionSpec as P

F32 = jnp.float32
BF16 = jnp.bfloat16


def whole(memory_space=pltpu.VMEM):
    return pl.BlockSpec(memory_space=memory_space)


def attend_kernel(len_ref, q_ref, k_hbm, v_hbm, o_ref, kbuf, vbuf, scr, sems, *, kv_heads):
    rows, heads, size = q_ref.shape
    per = heads // kv_heads

    def copies(t):
        return (
            pltpu.make_async_copy(k_hbm.at[t], kbuf.at[t], sems.at[0, t]),
            pltpu.make_async_copy(v_hbm.at[t], vbuf.at[t], sems.at[1, t]),
        )

    for t in range(rows):
        for c in copies(t):
            c.start()
    width = kbuf.shape[1]
    col = lax.broadcasted_iota(jnp.int32, (heads, width), 1)
    row = lax.broadcasted_iota(jnp.int32, (heads, width), 0)
    same = (col % kv_heads) == (row // per)
    slot = jnp.where(same, col // kv_heads, jnp.int32(2**30))
    for t in range(rows):
        kc, vc = copies(t)
        kc.wait()
        logits = lax.dot_general(
            q_ref[t], kbuf[t], (((1,), (1,)), ((), ())), preferred_element_type=F32
        ) * (1.0 / math.sqrt(size))
        logits = jnp.where(slot < len_ref[t], logits, -1e30)
        raised = jnp.exp(logits - jnp.max(logits, axis=1, keepdims=True))
        weights = (raised / jnp.sum(raised, axis=1, keepdims=True)).astype(BF16)
        vc.wait()
        scr[t * heads : (t + 1) * heads, :] = jnp.dot(weights, vbuf[t], preferred_element_type=F32)
    for j in range(heads):
        o_ref[:, j * size : (j + 1) * size] = scr[pl.ds(j, rows, stride=heads), :].astype(BF16)


def attend(queries, keys, values, lengths):
    rows, heads, size = queries.shape
    slots, kv_heads = keys.shape[1:3]
    flat = (rows, slots * kv_heads, size)
    return pl.pallas_call(
        functools.partial(attend_kernel, kv_heads=kv_heads),
        out_shape=jax.ShapeDtypeStruct((rows, heads * size), BF16),
        in_specs=[whole(pltpu.SMEM), whole(), whole(pl.ANY), whole(pl.ANY)],
        out_specs=whole(),
        scratch_shapes=[
            pltpu.VMEM(flat, BF16),
            pltpu.VMEM(flat, BF16),
            pltpu.VMEM((rows * heads, size), F32),
            pltpu.SemaphoreType.DMA((2, rows)),
        ],
        name="attend",
    )(lengths, queries, keys.reshape(flat), values.reshape(flat))


def project_kernel(src_ref, *refs, pieces, chunks):
    parts = refs[:pieces]
    w_hbm, o_ref, xs, wbuf, sems = refs[pieces:]
    depth = w_hbm.shape[0]
    step = depth // chunks

    def copy(c):
        sl = pl.ds(c * step, step)
        return pltpu.make_async_copy(w_hbm.at[sl], wbuf.at[sl], sems.at[c])

    for c in range(chunks):
        copy(c).start()
    loaded = [p[...].astype(F32) for p in parts]
    if pieces > 1:
        blocks = []
        for b in range(pieces):
            picked = loaded[0]
            for k in range(1, pieces):
                picked = jnp.where(src_ref[k] == b, loaded[k], picked)
            blocks.append(picked)
        x = jnp.concatenate(blocks, axis=0)
    else:
        x = loaded[0]
    xs[...] = x.astype(BF16)
    acc = None
    for c in range(chunks):
        copy(c).wait()
        sl = slice(c * step, (c + 1) * step)
        part = jnp.dot(xs[:, sl], wbuf[sl, :], preferred_element_type=F32)
        acc = part if acc is None else acc + part
    o_ref[...] = acc


def project(source, parts, out_weight, rows):
    depth, width = out_weight.shape
    chunks = 8
    return pl.pallas_call(
        functools.partial(project_kernel, pieces=len(parts), chunks=chunks),
        out_shape=jax.ShapeDtypeStruct((rows, width), F32),
        in_specs=[whole(pltpu.SMEM)] + [whole()] * len(parts) + [whole(pl.ANY)],
        out_specs=whole(),
        scratch_shapes=[
            pltpu.VMEM((rows, depth), BF16),
            pltpu.VMEM((depth, width), BF16),
            pltpu.SemaphoreType.DMA((chunks,)),
        ],
        name="project",
    )(source, *parts, out_weight)


def dispatch_kernel(own_ref, other_ref, resid_ref, sel_ref, hid_ref, out_ref):
    hidden = resid_ref[...].astype(F32) + (own_ref[...] + other_ref[...])
    hid_ref[...] = hidden
    out_ref[...] = jnp.dot(sel_ref[...], hidden.astype(BF16), preferred_element_type=F32).astype(BF16)


def dispatch(own, other, resid, selector):
    rows, width = resid.shape
    return pl.pallas_call(
        dispatch_kernel,
        out_shape=(
            jax.ShapeDtypeStruct((rows, width), F32),
            jax.ShapeDtypeStruct((selector.shape[0], width), BF16),
        ),
        in_specs=[whole()] * 4,
        out_specs=(whole(), whole()),
        name="dispatch",
    )(own, other, resid, selector)


def expert_kernel(x_ref, gain_ref, wg_hbm, wu_hbm, wd_hbm, o_ref, wbuf, dbuf, sems, dsems, *, groups, cols):
    items, width = x_ref.shape[1:]
    depth = cols * width
    hid = wg_hbm.shape[1]
    step = 512
    chunks = depth // step

    def copies(c):
        sl = pl.ds(c * step, step)
        return (
            pltpu.make_async_copy(wg_hbm.at[sl], wbuf.at[sl, pl.ds(0, hid)], sems.at[0, c]),
            pltpu.make_async_copy(wu_hbm.at[sl], wbuf.at[sl, pl.ds(hid, hid)], sems.at[1, c]),
        )

    down = pltpu.make_async_copy(wd_hbm, dbuf, dsems.at[0])
    for c in range(chunks):
        for d in copies(c):
            d.start()
    down.start()

    def column(e):
        return jnp.concatenate([x_ref[s * cols + e].astype(F32) for s in range(groups)], axis=0)

    squares = None
    for e in range(cols):
        x = column(e)
        part = jnp.sum(x * x, axis=1, keepdims=True)
        squares = part if squares is None else squares + part
    inverse = lax.rsqrt(squares / depth + 1e-06)
    normed = jnp.concatenate(
        [
            (column(e) * inverse * gain_ref[:, e * width : (e + 1) * width]).astype(BF16)
            for e in range(cols)
        ],
        axis=1,
    )
    acc = None
    for c in range(chunks):
        for d in copies(c):
            d.wait()
        sl = slice(c * step, (c + 1) * step)
        part = jnp.dot(normed[:, sl], wbuf[sl, :], preferred_element_type=F32)
        acc = part if acc is None else acc + part
    gate, up = acc[:, :hid], acc[:, hid:]
    activated = (gate / (1.0 + jnp.exp(-gate)) * up).astype(BF16)
    down.wait()
    for e in range(cols):
        y = jnp.dot(
            activated, dbuf[:, e * width : (e + 1) * width], preferred_element_type=F32
        ).astype(BF16)
        for s in range(groups):
            o_ref[s * cols + e] = y[s * items : (s + 1) * items, :]


def expert(arrived, gain, w_gate, w_up, w_down, groups, cols):
    depth, hid = w_gate.shape
    chunks = depth // 512
    return pl.pallas_call(
        functools.partial(expert_kernel, groups=groups, cols=cols),
        out_shape=jax.ShapeDtypeStruct(arrived.shape, BF16),
        in_specs=[whole(), whole(), whole(pl.ANY), whole(pl.ANY), whole(pl.ANY)],
        out_specs=whole(),
        scratch_shapes=[
            pltpu.VMEM((depth, 2 * hid), BF16),
            pltpu.VMEM((hid, depth), BF16),
            pltpu.SemaphoreType.DMA((2, chunks)),
            pltpu.SemaphoreType.DMA((1,)),
        ],
        name="expert",
    )(arrived, gain, w_gate, w_up, w_down)


def combine_kernel(spread_ref, y_ref, o_ref):
    rows = spread_ref.shape[0]
    spread = spread_ref[...]
    high = spread.astype(BF16)
    rest = spread - high.astype(F32)
    mid = rest.astype(BF16)
    low = (rest - mid.astype(F32)).astype(BF16)
    stacked = jnp.concatenate([high, mid, low], axis=0)
    res = jnp.dot(stacked, y_ref[...], preferred_element_type=F32)
    o_ref[...] = res[:rows] + (res[rows : 2 * rows] + res[2 * rows :])


def combine(spread, returned):
    return pl.pallas_call(
        combine_kernel,
        out_shape=jax.ShapeDtypeStruct((spread.shape[0], returned.shape[1]), F32),
        in_specs=[whole(), whole()],
        out_specs=whole(),
        name="combine",
    )(spread, returned)


def local(
    queries,
    keys,
    values,
    lengths,
    out_weight,
    resid,
    norm_gain,
    expert_ids,
    route_weights,
    w_gate,
    w_up,
    w_down,
):
    req_count = lax.axis_size("req")
    exp_count = lax.axis_size("exp")
    column = lax.axis_index("exp")
    rows_dev = queries.shape[0]
    group_rows, col_width = resid.shape
    capacity = 2 * rows_dev
    expert_total = req_count * exp_count

    def swap(x):
        return lax.ppermute(x, "head", [(0, 1), (1, 0)])

    attended = attend(queries, keys, values, lengths)
    if exp_count == 4:
        source = column ^ jnp.arange(exp_count, dtype=jnp.int32)
        parts = [attended] + [
            lax.ppermute(attended, "exp", [(i, i ^ k) for i in range(exp_count)])
            for k in range(1, exp_count)
        ]
    else:
        source = jnp.zeros((1,), jnp.int32)
        parts = [lax.all_gather(attended, "exp", axis=0, tiled=True)]

    matched = expert_ids[:, :, None] == jnp.arange(expert_total, dtype=jnp.int32)[None, None, :]
    chosen = jnp.any(matched, axis=1)
    weighting = jnp.sum(jnp.where(matched, route_weights[:, :, None], 0.0), axis=1)
    position = jnp.cumsum(chosen.astype(jnp.int32), axis=0) - 1
    selector = (
        position.T[:, None, :] == jnp.arange(capacity, dtype=jnp.int32)[None, :, None]
    ) & chosen.T[:, None, :]
    spread = jnp.where(selector, weighting.T[:, None, :], 0.0)
    spread = spread.reshape(expert_total * capacity, group_rows).T
    selector = selector.astype(BF16).reshape(expert_total * capacity, group_rows)

    own = project(source, parts, out_weight, group_rows)
    hidden, outgoing = dispatch(own, swap(own), resid, selector)
    outgoing = outgoing.reshape(expert_total, capacity, col_width)
    arrived = lax.all_to_all(outgoing, ("req", "exp"), split_axis=0, concat_axis=0, tiled=True)
    made = expert(
        arrived, norm_gain[None, :], w_gate[0], w_up[0], w_down[0], req_count, exp_count
    )
    returned = lax.all_to_all(made, ("req", "exp"), split_axis=0, concat_axis=0, tiled=True)
    mixture = combine(spread, returned.reshape(expert_total * capacity, col_width))
    return (hidden + (mixture + swap(mixture))).astype(BF16)


def solution(mesh):
    in_specs = (
        P(("req", "exp"), "head", None),
        P(("req", "exp"), None, "head", None),
        P(("req", "exp"), None, "head", None),
        P(("req", "exp")),
        P("head", "exp"),
        P("req", "exp"),
        P(),
        P("req", None),
        P("req", None),
        P(("req", "exp"), None, "head"),
        P(("req", "exp"), None, "head"),
        P(("req", "exp"), "head", None),
    )
    out_specs = P("req", "exp")
    return jax.shard_map(local, mesh=mesh, in_specs=in_specs, out_specs=out_specs, check_vma=False)
```

```python
import functools
import math

import jax
import jax.numpy as jnp
from jax import lax
from jax.experimental import pallas as pl
from jax.experimental.pallas import tpu as pltpu
from jax.sharding import PartitionSpec as P

F32 = jnp.float32
BF16 = jnp.bfloat16


def whole(memory_space=pltpu.VMEM):
    return pl.BlockSpec(memory_space=memory_space)


def near(x):
    return pltpu.with_memory_space_constraint(x, pltpu.VMEM)


def far(x):
    return pltpu.with_memory_space_constraint(x, pltpu.HBM)


def attend_kernel(
    len_hbm, q_hbm, k_hbm, v_hbm, w_hbm, o_ref, w_ref, len_ref, q_ref, kbuf, vbuf, scr, sems, one,
    *, kv_heads
):
    rows, heads, size = q_ref.shape
    per = heads // kv_heads

    def copies(t):
        return (
            pltpu.make_async_copy(k_hbm.at[t], kbuf.at[t], sems.at[0, t]),
            pltpu.make_async_copy(v_hbm.at[t], vbuf.at[t], sems.at[1, t]),
        )

    ask = pltpu.make_async_copy(q_hbm, q_ref, one.at[0])
    load = pltpu.make_async_copy(w_hbm, w_ref, one.at[1])
    span = pltpu.make_async_copy(len_hbm, len_ref, one.at[2])
    ask.start()
    span.start()
    for t in range(rows):
        for c in copies(t):
            c.start()
    load.start()
    width = kbuf.shape[1]
    col = lax.broadcasted_iota(jnp.int32, (heads, width), 1)
    row = lax.broadcasted_iota(jnp.int32, (heads, width), 0)
    same = (col % kv_heads) == (row // per)
    slot = jnp.where(same, col // kv_heads, jnp.int32(2**30))
    ask.wait()
    span.wait()
    for t in range(rows):
        kc, vc = copies(t)
        kc.wait()
        logits = lax.dot_general(
            q_ref[t], kbuf[t], (((1,), (1,)), ((), ())), preferred_element_type=F32
        ) * (1.0 / math.sqrt(size))
        logits = jnp.where(slot < len_ref[t], logits, -1e30)
        raised = jnp.exp(logits - jnp.max(logits, axis=1, keepdims=True))
        weights = (raised / jnp.sum(raised, axis=1, keepdims=True)).astype(BF16)
        vc.wait()
        scr[t * heads : (t + 1) * heads, :] = jnp.dot(weights, vbuf[t], preferred_element_type=F32)
    for j in range(heads):
        o_ref[:, j * size : (j + 1) * size] = scr[pl.ds(j, rows, stride=heads), :].astype(BF16)
    load.wait()


def attend(queries, keys, values, lengths, out_weight):
    rows, heads, size = queries.shape
    slots, kv_heads = keys.shape[1:3]
    flat = (rows, slots * kv_heads, size)
    return pl.pallas_call(
        functools.partial(attend_kernel, kv_heads=kv_heads),
        out_shape=(
            pltpu.VMEM((rows, heads * size), BF16),
            pltpu.VMEM(out_weight.shape, BF16),
        ),
        in_specs=[whole(pltpu.HBM)] * 5,
        out_specs=(whole(), whole()),
        scratch_shapes=[
            pltpu.SMEM((rows,), jnp.int32),
            pltpu.VMEM(queries.shape, BF16),
            pltpu.VMEM(flat, BF16),
            pltpu.VMEM(flat, BF16),
            pltpu.VMEM((rows * heads, size), F32),
            pltpu.SemaphoreType.DMA((2, rows)),
            pltpu.SemaphoreType.DMA((3,)),
        ],
        compiler_params=pltpu.CompilerParams(vmem_limit_bytes=16 * 2**20),
        name="attend",
    )(*map(far, (lengths, queries, keys.reshape(flat), values.reshape(flat), out_weight)))


def route_kernel(ids_ref, weight_ref, sel_ref, spread_ref, *, capacity):
    total, rows = sel_ref.shape
    experts = total // capacity
    expert = lax.broadcasted_iota(jnp.int32, (experts, rows), 0)
    chosen = jnp.zeros((experts, rows), F32)
    weight = jnp.zeros((experts, rows), F32)
    for k in range(ids_ref.shape[0]):
        hit = ids_ref[k : k + 1, :] == expert
        chosen = jnp.where(hit, 1.0, chosen)
        weight = weight + jnp.where(hit, weight_ref[k : k + 1, :], 0.0)
    before = lax.broadcasted_iota(jnp.int32, (rows, rows), 0)
    after = lax.broadcasted_iota(jnp.int32, (rows, rows), 1)
    upto = jnp.where(before <= after, 1.0, 0.0).astype(BF16)
    place = jnp.dot(chosen.astype(BF16), upto, preferred_element_type=F32) - 1.0
    place = jnp.where(chosen > 0.0, place, -1.0)
    seat = lax.broadcasted_iota(jnp.int32, (experts, capacity, rows), 1).astype(F32)
    taken = jnp.broadcast_to(place[:, None, :], seat.shape) == seat
    shares = jnp.where(taken, jnp.broadcast_to(weight[:, None, :], seat.shape), 0.0)
    sel_ref[...] = jnp.where(taken, 1.0, 0.0).reshape(total, rows).astype(BF16)
    spread_ref[...] = shares.reshape(total, rows).T


def route(expert_ids, route_weights, experts, capacity):
    rows = expert_ids.shape[0]
    total = experts * capacity
    return pl.pallas_call(
        functools.partial(route_kernel, capacity=capacity),
        out_shape=(pltpu.VMEM((total, rows), BF16), pltpu.VMEM((rows, total), F32)),
        in_specs=[whole(), whole()],
        out_specs=(whole(), whole()),
        compiler_params=pltpu.CompilerParams(vmem_limit_bytes=8 * 2**20),
        name="route",
    )(expert_ids.T, route_weights.T)


def project_kernel(*refs, pieces):
    parts = refs[:pieces]
    w_ref, wg_hbm, wu_hbm, wd_hbm, o_ref, both_ref, down_ref, sems = refs[pieces:]
    hid = wg_hbm.shape[1]
    loads = (
        pltpu.make_async_copy(wg_hbm, both_ref.at[:, pl.ds(0, hid)], sems.at[0]),
        pltpu.make_async_copy(wu_hbm, both_ref.at[:, pl.ds(hid, hid)], sems.at[1]),
        pltpu.make_async_copy(wd_hbm, down_ref, sems.at[2]),
    )
    for c in loads:
        c.start()
    loaded = [p[...].astype(F32) for p in parts]
    if pieces > 1:
        place = lax.axis_index("exp")
        blocks = []
        for b in range(pieces):
            picked = loaded[0]
            for k in range(1, pieces):
                picked = jnp.where((place ^ k) == b, loaded[k], picked)
            blocks.append(picked)
        x = jnp.concatenate(blocks, axis=0)
    else:
        x = loaded[0]
    o_ref[...] = jnp.dot(x.astype(BF16), w_ref[...], preferred_element_type=F32)
    for c in loads:
        c.wait()


def project(parts, out_weight, w_gate, w_up, w_down, rows):
    depth, hid = w_gate.shape
    return pl.pallas_call(
        functools.partial(project_kernel, pieces=len(parts)),
        out_shape=(
            pltpu.VMEM((rows, out_weight.shape[1]), F32),
            pltpu.VMEM((depth, 2 * hid), BF16),
            pltpu.VMEM(w_down.shape, BF16),
        ),
        in_specs=[whole()] * (len(parts) + 1) + [whole(pltpu.HBM)] * 3,
        out_specs=(whole(),) * 3,
        scratch_shapes=[pltpu.SemaphoreType.DMA((3,))],
        compiler_params=pltpu.CompilerParams(vmem_limit_bytes=8 * 2**20),
        name="project",
    )(*map(near, parts), near(out_weight), *map(far, (w_gate, w_up, w_down)))


def dispatch_kernel(own_ref, other_ref, resid_ref, sel_ref, hid_ref, out_ref):
    hidden = resid_ref[...].astype(F32) + (own_ref[...] + other_ref[...])
    hid_ref[...] = hidden
    out_ref[...] = jnp.dot(sel_ref[...], hidden.astype(BF16), preferred_element_type=F32).astype(BF16)


def dispatch(own, other, resid, selector):
    rows, width = resid.shape
    return pl.pallas_call(
        dispatch_kernel,
        out_shape=(
            pltpu.VMEM((rows, width), F32),
            pltpu.VMEM((selector.shape[0], width), BF16),
        ),
        in_specs=[whole()] * 4,
        out_specs=(whole(), whole()),
        compiler_params=pltpu.CompilerParams(vmem_limit_bytes=8 * 2**20),
        name="dispatch",
    )(near(own), near(other), near(resid), near(selector))


def expert_kernel(x_ref, gain_ref, both_ref, wd_ref, o_ref, *, groups, cols):
    items, width = x_ref.shape[1:]
    depth = cols * width
    hid = wd_ref.shape[0]

    def column(e):
        return jnp.concatenate([x_ref[s * cols + e].astype(F32) for s in range(groups)], axis=0)

    squares = None
    for e in range(cols):
        x = column(e)
        part = jnp.sum(x * x, axis=1, keepdims=True)
        squares = part if squares is None else squares + part
    inverse = lax.rsqrt(squares / depth + 1e-06)
    acc = None
    for e in range(cols):
        sl = slice(e * width, (e + 1) * width)
        normed = (column(e) * inverse * gain_ref[:, sl]).astype(BF16)
        part = jnp.dot(normed, both_ref[sl, :], preferred_element_type=F32)
        acc = part if acc is None else acc + part
    gate, up = acc[:, :hid], acc[:, hid:]
    activated = (gate / (1.0 + jnp.exp(-gate)) * up).astype(BF16)
    for e in range(cols):
        y = jnp.dot(
            activated, wd_ref[:, e * width : (e + 1) * width], preferred_element_type=F32
        ).astype(BF16)
        for s in range(groups):
            o_ref[s * cols + e] = y[s * items : (s + 1) * items, :]


def expert(arrived, gain, both, down, groups, cols):
    return pl.pallas_call(
        functools.partial(expert_kernel, groups=groups, cols=cols),
        out_shape=pltpu.VMEM(arrived.shape, BF16),
        in_specs=[whole()] * 4,
        out_specs=whole(),
        compiler_params=pltpu.CompilerParams(vmem_limit_bytes=12 * 2**20),
        name="expert",
    )(*map(near, (arrived, gain, both, down)))


def combine_kernel(spread_ref, y_ref, o_ref):
    rows = spread_ref.shape[0]
    spread = spread_ref[...]
    high = spread.astype(BF16)
    rest = spread - high.astype(F32)
    mid = rest.astype(BF16)
    low = (rest - mid.astype(F32)).astype(BF16)
    stacked = jnp.concatenate([high, mid, low], axis=0)
    res = jnp.dot(stacked, y_ref[...], preferred_element_type=F32)
    o_ref[...] = res[:rows] + (res[rows : 2 * rows] + res[2 * rows :])


def combine(spread, returned):
    return pl.pallas_call(
        combine_kernel,
        out_shape=pltpu.VMEM((spread.shape[0], returned.shape[1]), F32),
        in_specs=[whole(), whole()],
        out_specs=whole(),
        compiler_params=pltpu.CompilerParams(vmem_limit_bytes=8 * 2**20),
        name="combine",
    )(near(spread), near(returned))


def local(
    queries,
    keys,
    values,
    lengths,
    out_weight,
    resid,
    norm_gain,
    expert_ids,
    route_weights,
    w_gate,
    w_up,
    w_down,
):
    req_count = lax.axis_size("req")
    exp_count = lax.axis_size("exp")
    rows_dev = queries.shape[0]
    group_rows, col_width = resid.shape
    capacity = 2 * rows_dev
    expert_total = req_count * exp_count

    def swap(x):
        return lax.ppermute(x, "head", [(0, 1), (1, 0)])

    attended, near_weight = attend(queries, keys, values, lengths, out_weight)
    if exp_count == 4:
        parts = [attended] + [
            lax.ppermute(attended, "exp", [(i, i ^ k) for i in range(exp_count)])
            for k in range(1, exp_count)
        ]
    else:
        parts = [lax.all_gather(attended, "exp", axis=0, tiled=True)]

    selector, spread = route(expert_ids, route_weights, expert_total, capacity)
    parts, selector, spread = lax.optimization_barrier((parts, selector, spread))
    own, both, down = project(parts, near_weight, w_gate[0], w_up[0], w_down[0], group_rows)
    hidden, outgoing = dispatch(own, swap(own), resid, selector)
    outgoing = outgoing.reshape(expert_total, capacity, col_width)
    arrived = lax.all_to_all(outgoing, ("req", "exp"), split_axis=0, concat_axis=0, tiled=True)
    made = expert(arrived, norm_gain[None, :], both, down, req_count, exp_count)
    returned = lax.all_to_all(made, ("req", "exp"), split_axis=0, concat_axis=0, tiled=True)
    mixture = combine(spread, returned.reshape(expert_total * capacity, col_width))
    return (hidden + (mixture + swap(mixture))).astype(BF16)


def solution(mesh):
    in_specs = (
        P(("req", "exp"), "head", None),
        P(("req", "exp"), None, "head", None),
        P(("req", "exp"), None, "head", None),
        P(("req", "exp")),
        P("head", "exp"),
        P("req", "exp"),
        P(),
        P("req", None),
        P("req", None),
        P(("req", "exp"), None, "head"),
        P(("req", "exp"), None, "head"),
        P(("req", "exp"), "head", None),
    )
    out_specs = P("req", "exp")
    return jax.shard_map(local, mesh=mesh, in_specs=in_specs, out_specs=out_specs, check_vma=False)
```

```python
import functools
import math

import jax
import jax.numpy as jnp
from jax import lax
from jax.experimental import pallas as pl
from jax.experimental.pallas import tpu as pltpu
from jax.sharding import PartitionSpec as P

F32 = jnp.float32
BF16 = jnp.bfloat16


def whole(memory_space=pltpu.VMEM):
    return pl.BlockSpec(memory_space=memory_space)


def near(x):
    return pltpu.with_memory_space_constraint(x, pltpu.VMEM)


def far(x):
    return pltpu.with_memory_space_constraint(x, pltpu.HBM)


def attend_kernel(
    len_hbm, q_hbm, k_hbm, v_hbm, w_hbm, o_ref, w_ref, len_ref, q_ref, kbuf, vbuf, scr, sems, one,
    *, kv_heads
):
    rows, heads, size = q_ref.shape
    per = heads // kv_heads

    def copies(t):
        return (
            pltpu.make_async_copy(k_hbm.at[t], kbuf.at[t], sems.at[0, t]),
            pltpu.make_async_copy(v_hbm.at[t], vbuf.at[t], sems.at[1, t]),
        )

    ask = pltpu.make_async_copy(q_hbm, q_ref, one.at[0])
    span = pltpu.make_async_copy(len_hbm, len_ref, one.at[1])
    load = pltpu.make_async_copy(w_hbm.at[pl.ds(0, w_ref.shape[0])], w_ref, one.at[2])
    ask.start()
    span.start()
    for t in range(rows):
        for c in copies(t):
            c.start()
    load.start()
    width = kbuf.shape[1]
    col = lax.broadcasted_iota(jnp.int32, (heads, width), 1)
    row = lax.broadcasted_iota(jnp.int32, (heads, width), 0)
    same = (col % kv_heads) == (row // per)
    slot = jnp.where(same, col // kv_heads, jnp.int32(2**30))
    ask.wait()
    span.wait()
    for t in range(rows):
        kc, vc = copies(t)
        kc.wait()
        logits = lax.dot_general(
            q_ref[t], kbuf[t], (((1,), (1,)), ((), ())), preferred_element_type=F32
        ) * (1.0 / math.sqrt(size))
        logits = jnp.where(slot < len_ref[t], logits, -1e30)
        raised = jnp.exp(logits - jnp.max(logits, axis=1, keepdims=True))
        weights = (raised / jnp.sum(raised, axis=1, keepdims=True)).astype(BF16)
        vc.wait()
        scr[t * heads : (t + 1) * heads, :] = jnp.dot(weights, vbuf[t], preferred_element_type=F32)
    for j in range(heads):
        o_ref[:, j * size : (j + 1) * size] = scr[pl.ds(j, rows, stride=heads), :].astype(BF16)
    load.wait()


def attend(queries, keys, values, lengths, out_weight, early):
    rows, heads, size = queries.shape
    slots, kv_heads = keys.shape[1:3]
    flat = (rows, slots * kv_heads, size)
    return pl.pallas_call(
        functools.partial(attend_kernel, kv_heads=kv_heads),
        out_shape=(
            pltpu.VMEM((rows, heads * size), BF16),
            pltpu.VMEM((early, out_weight.shape[1]), BF16),
        ),
        in_specs=[whole(pltpu.HBM)] * 5,
        out_specs=(whole(), whole()),
        scratch_shapes=[
            pltpu.SMEM((rows,), jnp.int32),
            pltpu.VMEM(queries.shape, BF16),
            pltpu.VMEM(flat, BF16),
            pltpu.VMEM(flat, BF16),
            pltpu.VMEM((rows * heads, size), F32),
            pltpu.SemaphoreType.DMA((2, rows)),
            pltpu.SemaphoreType.DMA((3,)),
        ],
        compiler_params=pltpu.CompilerParams(vmem_limit_bytes=8 * 2**20),
        name="attend",
    )(*map(far, (lengths, queries, keys.reshape(flat), values.reshape(flat), out_weight)))


def stage_kernel(
    ids_hbm, weight_hbm, resid_hbm, gain_hbm, w_hbm,
    sel_ref, spread_ref, resid_ref, gain_ref, w_ref, ids_ref, weight_ref, sems,
    *, capacity,
):
    tail = w_hbm.at[pl.ds(w_hbm.shape[0] - w_ref.shape[0], w_ref.shape[0])]
    pairs = (
        (ids_hbm, ids_ref),
        (weight_hbm, weight_ref),
        (tail, w_ref),
        (resid_hbm, resid_ref),
        (gain_hbm, gain_ref),
    )
    loads = [pltpu.make_async_copy(a, b, sems.at[i]) for i, (a, b) in enumerate(pairs)]
    for c in loads:
        c.start()
    total, rows = sel_ref.shape
    experts = total // capacity
    loads[0].wait()
    loads[1].wait()
    expert = lax.broadcasted_iota(jnp.int32, (experts, rows), 0)
    chosen = jnp.zeros((experts, rows), F32)
    weight = jnp.zeros((experts, rows), F32)
    for k in range(ids_ref.shape[0]):
        hit = ids_ref[k : k + 1, :] == expert
        chosen = jnp.where(hit, 1.0, chosen)
        weight = weight + jnp.where(hit, weight_ref[k : k + 1, :], 0.0)
    before = lax.broadcasted_iota(jnp.int32, (rows, rows), 0)
    after = lax.broadcasted_iota(jnp.int32, (rows, rows), 1)
    upto = jnp.where(before <= after, 1.0, 0.0).astype(BF16)
    place = jnp.dot(chosen.astype(BF16), upto, preferred_element_type=F32) - 1.0
    place = jnp.where(chosen > 0.0, place, -1.0)
    seat = lax.broadcasted_iota(jnp.int32, (experts, capacity, rows), 1).astype(F32)
    taken = jnp.broadcast_to(place[:, None, :], seat.shape) == seat
    shares = jnp.where(taken, jnp.broadcast_to(weight[:, None, :], seat.shape), 0.0)
    sel_ref[...] = jnp.where(taken, 1.0, 0.0).reshape(total, rows).astype(BF16)
    spread_ref[...] = shares.reshape(total, rows).T
    for c in loads[2:]:
        c.wait()


def stage(expert_ids, route_weights, resid, gain, out_weight, experts, capacity, early):
    rows, top = expert_ids.shape
    total = experts * capacity
    depth, width = out_weight.shape
    return pl.pallas_call(
        functools.partial(stage_kernel, capacity=capacity),
        out_shape=(
            pltpu.VMEM((total, rows), BF16),
            pltpu.VMEM((rows, total), F32),
            pltpu.VMEM(resid.shape, BF16),
            pltpu.VMEM(gain.shape, F32),
            pltpu.VMEM((depth - early, width), BF16),
        ),
        in_specs=[whole(pltpu.HBM)] * 5,
        out_specs=(whole(),) * 5,
        scratch_shapes=[
            pltpu.VMEM((top, rows), jnp.int32),
            pltpu.VMEM((top, rows), F32),
            pltpu.SemaphoreType.DMA((5,)),
        ],
        compiler_params=pltpu.CompilerParams(vmem_limit_bytes=8 * 2**20),
        name="stage",
    )(*map(far, (expert_ids.T, route_weights.T, resid, gain, out_weight)))


def project_kernel(*refs, pieces):
    parts = refs[:pieces]
    first_ref, second_ref, o_ref = refs[pieces:]
    early = first_ref.shape[0]
    loaded = [p[...].astype(F32) for p in parts]
    if pieces > 1:
        place = lax.axis_index("exp")
        blocks = []
        for b in range(pieces):
            picked = loaded[0]
            for k in range(1, pieces):
                picked = jnp.where((place ^ k) == b, loaded[k], picked)
            blocks.append(picked)
        x = jnp.concatenate(blocks, axis=0)
    else:
        x = loaded[0]
    x = x.astype(BF16)
    o_ref[...] = jnp.dot(x[:, :early], first_ref[...], preferred_element_type=F32) + jnp.dot(
        x[:, early:], second_ref[...], preferred_element_type=F32
    )


def project(parts, first, second, rows):
    width = first.shape[1]
    return pl.pallas_call(
        functools.partial(project_kernel, pieces=len(parts)),
        out_shape=pltpu.VMEM((rows, width), F32),
        in_specs=[whole()] * (len(parts) + 2),
        out_specs=whole(),
        compiler_params=pltpu.CompilerParams(vmem_limit_bytes=8 * 2**20),
        name="project",
    )(*map(near, parts), near(first), near(second))


def dispatch_kernel(own_ref, other_ref, resid_ref, sel_ref, hid_ref, out_ref):
    hidden = resid_ref[...].astype(F32) + (own_ref[...] + other_ref[...])
    hid_ref[...] = hidden
    out_ref[...] = jnp.dot(sel_ref[...], hidden.astype(BF16), preferred_element_type=F32).astype(BF16)


def dispatch(own, other, resid, selector):
    rows, width = resid.shape
    return pl.pallas_call(
        dispatch_kernel,
        out_shape=(
            pltpu.VMEM((rows, width), F32),
            pltpu.VMEM((selector.shape[0], width), BF16),
        ),
        in_specs=[whole()] * 4,
        out_specs=(whole(), whole()),
        compiler_params=pltpu.CompilerParams(vmem_limit_bytes=8 * 2**20),
        name="dispatch",
    )(near(own), near(other), near(resid), near(selector))


def expert_kernel(x_ref, gain_ref, wg_ref, wu_ref, wd_ref, o_ref, *, groups, cols):
    items, width = x_ref.shape[1:]
    depth = cols * width
    hid = wd_ref.shape[0]

    def column(e):
        return jnp.concatenate([x_ref[s * cols + e].astype(F32) for s in range(groups)], axis=0)

    squares = None
    for e in range(cols):
        x = column(e)
        part = jnp.sum(x * x, axis=1, keepdims=True)
        squares = part if squares is None else squares + part
    inverse = lax.rsqrt(squares / depth + 1e-06)
    acc = None
    for e in range(cols):
        sl = slice(e * width, (e + 1) * width)
        normed = (column(e) * inverse * gain_ref[:, sl]).astype(BF16)
        both = jnp.concatenate([wg_ref[sl, :], wu_ref[sl, :]], axis=1)
        part = jnp.dot(normed, both, preferred_element_type=F32)
        acc = part if acc is None else acc + part
    gate, up = acc[:, :hid], acc[:, hid:]
    activated = (gate / (1.0 + jnp.exp(-gate)) * up).astype(BF16)
    for e in range(cols):
        y = jnp.dot(
            activated, wd_ref[:, e * width : (e + 1) * width], preferred_element_type=F32
        ).astype(BF16)
        for s in range(groups):
            o_ref[s * cols + e] = y[s * items : (s + 1) * items, :]


def expert(arrived, gain, w_gate, w_up, w_down, groups, cols):
    return pl.pallas_call(
        functools.partial(expert_kernel, groups=groups, cols=cols),
        out_shape=pltpu.VMEM(arrived.shape, BF16),
        in_specs=[whole()] * 5,
        out_specs=whole(),
        compiler_params=pltpu.CompilerParams(vmem_limit_bytes=12 * 2**20),
        name="expert",
    )(near(arrived), near(gain), near(w_gate), near(w_up), near(w_down))


def combine_kernel(spread_ref, y_ref, o_ref):
    rows = spread_ref.shape[0]
    spread = spread_ref[...]
    high = spread.astype(BF16)
    rest = spread - high.astype(F32)
    mid = rest.astype(BF16)
    low = (rest - mid.astype(F32)).astype(BF16)
    stacked = jnp.concatenate([high, mid, low], axis=0)
    res = jnp.dot(stacked, y_ref[...], preferred_element_type=F32)
    o_ref[...] = res[:rows] + (res[rows : 2 * rows] + res[2 * rows :])


def combine(spread, returned):
    return pl.pallas_call(
        combine_kernel,
        out_shape=pltpu.VMEM((spread.shape[0], returned.shape[1]), F32),
        in_specs=[whole(), whole()],
        out_specs=whole(),
        compiler_params=pltpu.CompilerParams(vmem_limit_bytes=8 * 2**20),
        name="combine",
    )(near(spread), near(returned))


def local(
    queries,
    keys,
    values,
    lengths,
    out_weight,
    resid,
    norm_gain,
    expert_ids,
    route_weights,
    w_gate,
    w_up,
    w_down,
):
    req_count = lax.axis_size("req")
    exp_count = lax.axis_size("exp")
    rows_dev = queries.shape[0]
    group_rows, col_width = resid.shape
    capacity = 2 * rows_dev
    expert_total = req_count * exp_count

    def swap(x):
        return lax.ppermute(x, "head", [(0, 1), (1, 0)])

    early = out_weight.shape[0] * 3 // 8
    attended, first = attend(queries, keys, values, lengths, out_weight, early)
    if exp_count == 4:
        parts = [attended] + [
            lax.ppermute(attended, "exp", [(i, i ^ k) for i in range(exp_count)])
            for k in range(1, exp_count)
        ]
    else:
        parts = [lax.all_gather(attended, "exp", axis=0, tiled=True)]

    staged = stage(
        expert_ids, route_weights, resid, norm_gain[None, :], out_weight, expert_total, capacity, early
    )
    parts, staged = lax.optimization_barrier((parts, staged))
    selector, spread, near_resid, near_gain, second = staged
    own = project(parts, first, second, group_rows)
    hidden, outgoing = dispatch(own, swap(own), near_resid, selector)
    outgoing = outgoing.reshape(expert_total, capacity, col_width)
    arrived = lax.all_to_all(outgoing, ("req", "exp"), split_axis=0, concat_axis=0, tiled=True)
    made = expert(
        arrived, near_gain, w_gate[0], w_up[0], w_down[0], req_count, exp_count
    )
    returned = lax.all_to_all(made, ("req", "exp"), split_axis=0, concat_axis=0, tiled=True)
    mixture = combine(spread, returned.reshape(expert_total * capacity, col_width))
    return (hidden + (mixture + swap(mixture))).astype(BF16)


def solution(mesh):
    in_specs = (
        P(("req", "exp"), "head", None),
        P(("req", "exp"), None, "head", None),
        P(("req", "exp"), None, "head", None),
        P(("req", "exp")),
        P("head", "exp"),
        P("req", "exp"),
        P(),
        P("req", None),
        P("req", None),
        P(("req", "exp"), None, "head"),
        P(("req", "exp"), None, "head"),
        P(("req", "exp"), "head", None),
    )
    out_specs = P("req", "exp")
    return jax.shard_map(local, mesh=mesh, in_specs=in_specs, out_specs=out_specs, check_vma=False)
```

```python
import functools
import math

import jax
import jax.numpy as jnp
from jax import lax
from jax.experimental import pallas as pl
from jax.experimental.pallas import tpu as pltpu
from jax.sharding import PartitionSpec as P

F32 = jnp.float32
BF16 = jnp.bfloat16


def whole(memory_space=pltpu.VMEM):
    return pl.BlockSpec(memory_space=memory_space)


def near(x):
    return pltpu.with_memory_space_constraint(x, pltpu.VMEM)


def far(x):
    return pltpu.with_memory_space_constraint(x, pltpu.HBM)


def attend_kernel(
    len_hbm, q_hbm, k_hbm, v_hbm, w_hbm, o_ref, w_ref, len_ref, q_ref, kbuf, vbuf, scr, sems, one,
    *, kv_heads
):
    rows, heads, size = q_ref.shape
    width = kbuf.shape[1]
    per = heads // kv_heads
    tile = 128
    tiles = width // tile
    ask = pltpu.make_async_copy(q_hbm, q_ref, one.at[0])
    span = pltpu.make_async_copy(len_hbm, len_ref, one.at[1])
    load = pltpu.make_async_copy(w_hbm.at[pl.ds(0, w_ref.shape[0])], w_ref, one.at[2])
    kcs = [pltpu.make_async_copy(k_hbm.at[t], kbuf.at[t], sems.at[0, t]) for t in range(rows)]
    vcs = [pltpu.make_async_copy(v_hbm.at[t], vbuf.at[t], sems.at[1, t]) for t in range(rows)]
    for c in [ask, span] + kcs + vcs + [load]:
        c.start()
    lane = lax.broadcasted_iota(jnp.int32, (per, tile), 1)
    group = lane % kv_heads
    slot = lane // kv_heads
    rate = math.log2(math.e) / math.sqrt(size)

    def grouped(fold, unit, reduce):
        res = jnp.zeros((per, tile), F32)
        for g in range(kv_heads):
            one_g = reduce(jnp.where(group == g, fold, unit), axis=1, keepdims=True)
            res = jnp.where(group == g, one_g, res)
        return res

    ask.wait()
    span.wait()
    for c in kcs:
        c.wait()
    weights = []
    for t in range(rows):
        full = lax.dot_general(
            q_ref[t], kbuf[t], (((1,), (1,)), ((), ())), preferred_element_type=F32
        )
        parts = []
        for i in range(tiles):
            cut = slice(i * tile, (i + 1) * tile)
            mine = full[:per, cut]
            for g in range(1, kv_heads):
                mine = jnp.where(group == g, full[g * per : (g + 1) * per, cut], mine)
            live = slot < len_ref[t] - i * (tile // kv_heads)
            parts.append(jnp.where(live, mine, -1e30))
        top = grouped(functools.reduce(jnp.maximum, parts), -1e30, jnp.max)
        raised = [jnp.exp2((p - top) * rate) for p in parts]
        share = 1.0 / grouped(functools.reduce(jnp.add, raised), 0.0, jnp.sum)
        soft = [(r * share).astype(BF16) for r in raised]
        weights.append(
            jnp.concatenate(
                [
                    jnp.concatenate([jnp.where(group == g, w, jnp.zeros_like(w)) for w in soft], axis=1)
                    for g in range(kv_heads)
                ],
                axis=0,
            )
        )
    for c in vcs:
        c.wait()
    for t in range(rows):
        scr[t * heads : (t + 1) * heads, :] = jnp.dot(
            weights[t], vbuf[t], preferred_element_type=F32
        )
    for j in range(heads):
        o_ref[:, j * size : (j + 1) * size] = scr[pl.ds(j, rows, stride=heads), :].astype(BF16)
    load.wait()


def attend(queries, keys, values, lengths, out_weight, early):
    rows, heads, size = queries.shape
    slots, kv_heads = keys.shape[1:3]
    flat = (rows, slots * kv_heads, size)
    return pl.pallas_call(
        functools.partial(attend_kernel, kv_heads=kv_heads),
        out_shape=(
            pltpu.VMEM((rows, heads * size), BF16),
            pltpu.VMEM((early, out_weight.shape[1]), BF16),
        ),
        in_specs=[whole(pltpu.HBM)] * 5,
        out_specs=(whole(), whole()),
        scratch_shapes=[
            pltpu.SMEM((rows,), jnp.int32),
            pltpu.VMEM(queries.shape, BF16),
            pltpu.VMEM(flat, BF16),
            pltpu.VMEM(flat, BF16),
            pltpu.VMEM((rows * heads, size), F32),
            pltpu.SemaphoreType.DMA((2, rows)),
            pltpu.SemaphoreType.DMA((3,)),
        ],
        compiler_params=pltpu.CompilerParams(vmem_limit_bytes=8 * 2**20),
        name="attend",
    )(*map(far, (lengths, queries, keys.reshape(flat), values.reshape(flat), out_weight)))


def stage_kernel(
    ids_hbm, weight_hbm, resid_hbm, gain_hbm, w_hbm,
    sel_ref, spread_ref, resid_ref, gain_ref, w_ref, ids_ref, weight_ref, sems,
    *, capacity,
):
    tail = w_hbm.at[pl.ds(w_hbm.shape[0] - w_ref.shape[0], w_ref.shape[0])]
    pairs = (
        (ids_hbm, ids_ref),
        (weight_hbm, weight_ref),
        (tail, w_ref),
        (resid_hbm, resid_ref),
        (gain_hbm, gain_ref),
    )
    loads = [pltpu.make_async_copy(a, b, sems.at[i]) for i, (a, b) in enumerate(pairs)]
    for c in loads:
        c.start()
    total, rows = sel_ref.shape
    experts = total // capacity
    loads[0].wait()
    loads[1].wait()
    expert = lax.broadcasted_iota(jnp.int32, (experts, rows), 0)
    chosen = jnp.zeros((experts, rows), F32)
    weight = jnp.zeros((experts, rows), F32)
    for k in range(ids_ref.shape[0]):
        hit = ids_ref[k : k + 1, :] == expert
        chosen = jnp.where(hit, 1.0, chosen)
        weight = weight + jnp.where(hit, weight_ref[k : k + 1, :], 0.0)
    before = lax.broadcasted_iota(jnp.int32, (rows, rows), 0)
    after = lax.broadcasted_iota(jnp.int32, (rows, rows), 1)
    upto = jnp.where(before <= after, 1.0, 0.0).astype(BF16)
    place = jnp.dot(chosen.astype(BF16), upto, preferred_element_type=F32) - 1.0
    place = jnp.where(chosen > 0.0, place, -1.0)
    seat = lax.broadcasted_iota(jnp.int32, (experts, capacity, rows), 1).astype(F32)
    taken = jnp.broadcast_to(place[:, None, :], seat.shape) == seat
    shares = jnp.where(taken, jnp.broadcast_to(weight[:, None, :], seat.shape), 0.0)
    sel_ref[...] = jnp.where(taken, 1.0, 0.0).reshape(total, rows).astype(BF16)
    spread_ref[...] = shares.reshape(total, rows).T
    for c in loads[2:]:
        c.wait()


def stage(expert_ids, route_weights, resid, gain, out_weight, experts, capacity, early):
    rows, top = expert_ids.shape
    total = experts * capacity
    depth, width = out_weight.shape
    return pl.pallas_call(
        functools.partial(stage_kernel, capacity=capacity),
        out_shape=(
            pltpu.VMEM((total, rows), BF16),
            pltpu.VMEM((rows, total), F32),
            pltpu.VMEM(resid.shape, BF16),
            pltpu.VMEM(gain.shape, F32),
            pltpu.VMEM((depth - early, width), BF16),
        ),
        in_specs=[whole(pltpu.HBM)] * 5,
        out_specs=(whole(),) * 5,
        scratch_shapes=[
            pltpu.VMEM((top, rows), jnp.int32),
            pltpu.VMEM((top, rows), F32),
            pltpu.SemaphoreType.DMA((5,)),
        ],
        compiler_params=pltpu.CompilerParams(vmem_limit_bytes=8 * 2**20),
        name="stage",
    )(*map(far, (expert_ids.T, route_weights.T, resid, gain, out_weight)))


def project_kernel(*refs, pieces):
    parts = refs[:pieces]
    first_ref, second_ref, keep_ref, give_ref = refs[pieces:]
    early = first_ref.shape[0]
    loaded = [p[...].astype(F32) for p in parts]
    if pieces > 1:
        place = lax.axis_index("exp")
        blocks = []
        for b in range(pieces):
            picked = loaded[0]
            for k in range(1, pieces):
                picked = jnp.where((place ^ k) == b, loaded[k], picked)
            blocks.append(picked)
        x = jnp.concatenate(blocks, axis=0)
    else:
        x = loaded[0]
    x = x.astype(BF16)
    res = jnp.dot(x[:, :early], first_ref[...], preferred_element_type=F32) + jnp.dot(
        x[:, early:], second_ref[...], preferred_element_type=F32
    )
    half = keep_ref.shape[1]
    low = lax.axis_index("head") == 0
    keep_ref[...] = jnp.where(low, res[:, :half], res[:, half:])
    give_ref[...] = jnp.where(low, res[:, half:], res[:, :half])


def project(parts, first, second, rows):
    half = first.shape[1] // 2
    return pl.pallas_call(
        functools.partial(project_kernel, pieces=len(parts)),
        out_shape=(pltpu.VMEM((rows, half), F32),) * 2,
        in_specs=[whole()] * (len(parts) + 2),
        out_specs=(whole(), whole()),
        compiler_params=pltpu.CompilerParams(vmem_limit_bytes=8 * 2**20),
        name="project",
    )(*map(near, parts), near(first), near(second))


def dispatch_kernel(own_ref, other_ref, resid_ref, sel_ref, hid_ref, out_ref):
    half = own_ref.shape[1]
    resid = jnp.where(lax.axis_index("head") == 0, resid_ref[:, :half], resid_ref[:, half:])
    hidden = resid.astype(F32) + (own_ref[...] + other_ref[...])
    hid_ref[...] = hidden
    out_ref[...] = jnp.dot(sel_ref[...], hidden.astype(BF16), preferred_element_type=F32).astype(BF16)


def dispatch(own, other, resid, selector):
    rows, half = own.shape
    return pl.pallas_call(
        dispatch_kernel,
        out_shape=(
            pltpu.VMEM((rows, half), F32),
            pltpu.VMEM((selector.shape[0], half), BF16),
        ),
        in_specs=[whole()] * 4,
        out_specs=(whole(), whole()),
        compiler_params=pltpu.CompilerParams(vmem_limit_bytes=8 * 2**20),
        name="dispatch",
    )(near(own), near(other), near(resid), near(selector))


def expert_kernel(
    own_ref, other_ref, gain_ref, wg_ref, wu_ref, wd_ref, keep_ref, give_ref, *, groups, cols
):
    items, half = own_ref.shape[1:]
    depth = 2 * cols * half
    hid = wd_ref.shape[0]
    low = lax.axis_index("head") == 0

    def column(e, lower):
        picks = []
        for s in range(groups):
            a = own_ref[s * cols + e].astype(F32)
            b = other_ref[s * cols + e].astype(F32)
            picks.append(jnp.where(low, a, b) if lower else jnp.where(low, b, a))
        return jnp.concatenate(picks, axis=0)

    squares = None
    for e in range(cols):
        for lower in (True, False):
            x = column(e, lower)
            part = jnp.sum(x * x, axis=1, keepdims=True)
            squares = part if squares is None else squares + part
    inverse = lax.rsqrt(squares / depth + 1e-06)
    acc = None
    for e in range(cols):
        for i, lower in enumerate((True, False)):
            sl = slice((2 * e + i) * half, (2 * e + i + 1) * half)
            normed = (column(e, lower) * inverse * gain_ref[:, sl]).astype(BF16)
            both = jnp.concatenate([wg_ref[sl, :], wu_ref[sl, :]], axis=1)
            part = jnp.dot(normed, both, preferred_element_type=F32)
            acc = part if acc is None else acc + part
    gate, up = acc[:, :hid], acc[:, hid:]
    activated = (gate / (1.0 + jnp.exp(-gate)) * up).astype(BF16)
    for e in range(cols):
        y = jnp.dot(
            activated, wd_ref[:, 2 * e * half : 2 * (e + 1) * half], preferred_element_type=F32
        )
        keep = jnp.where(low, y[:, :half], y[:, half:])
        give = jnp.where(low, y[:, half:], y[:, :half]).astype(BF16)
        for s in range(groups):
            keep_ref[s * cols + e] = keep[s * items : (s + 1) * items, :]
            give_ref[s * cols + e] = give[s * items : (s + 1) * items, :]


def expert(own, other, gain, w_gate, w_up, w_down, groups, cols):
    return pl.pallas_call(
        functools.partial(expert_kernel, groups=groups, cols=cols),
        out_shape=(pltpu.VMEM(own.shape, F32), pltpu.VMEM(own.shape, BF16)),
        in_specs=[whole()] * 6,
        out_specs=(whole(), whole()),
        compiler_params=pltpu.CompilerParams(vmem_limit_bytes=12 * 2**20),
        name="expert",
    )(*map(near, (own, other, gain, w_gate, w_up, w_down)))


def merge_kernel(keep_ref, got_ref, o_ref):
    o_ref[...] = (keep_ref[...] + got_ref[...].astype(F32)).astype(BF16)


def merge(keep, got):
    return pl.pallas_call(
        merge_kernel,
        out_shape=pltpu.VMEM(keep.shape, BF16),
        in_specs=[whole(), whole()],
        out_specs=whole(),
        compiler_params=pltpu.CompilerParams(vmem_limit_bytes=8 * 2**20),
        name="merge",
    )(near(keep), near(got))


def combine_kernel(spread_ref, y_ref, hid_ref, o_ref):
    rows = spread_ref.shape[0]
    spread = spread_ref[...]
    high = spread.astype(BF16)
    rest = spread - high.astype(F32)
    mid = rest.astype(BF16)
    low = (rest - mid.astype(F32)).astype(BF16)
    stacked = jnp.concatenate([high, mid, low], axis=0)
    res = jnp.dot(stacked, y_ref[...], preferred_element_type=F32)
    mixture = res[:rows] + (res[rows : 2 * rows] + res[2 * rows :])
    o_ref[...] = (hid_ref[...] + mixture).astype(BF16)


def combine(spread, returned, hidden):
    return pl.pallas_call(
        combine_kernel,
        out_shape=pltpu.VMEM(hidden.shape, BF16),
        in_specs=[whole()] * 3,
        out_specs=whole(),
        compiler_params=pltpu.CompilerParams(vmem_limit_bytes=8 * 2**20),
        name="combine",
    )(near(spread), near(returned), near(hidden))


def join_kernel(own_ref, other_ref, o_ref):
    half = own_ref.shape[1]
    low = lax.axis_index("head") == 0
    o_ref[:, :half] = jnp.where(low, own_ref[...], other_ref[...])
    o_ref[:, half:] = jnp.where(low, other_ref[...], own_ref[...])


def join(own, other):
    rows, half = own.shape
    return pl.pallas_call(
        join_kernel,
        out_shape=jax.ShapeDtypeStruct((rows, 2 * half), BF16),
        in_specs=[whole(), whole()],
        out_specs=whole(),
        compiler_params=pltpu.CompilerParams(vmem_limit_bytes=8 * 2**20),
        name="join",
    )(near(own), near(other))


def local(
    queries,
    keys,
    values,
    lengths,
    out_weight,
    resid,
    norm_gain,
    expert_ids,
    route_weights,
    w_gate,
    w_up,
    w_down,
):
    req_count = lax.axis_size("req")
    exp_count = lax.axis_size("exp")
    rows_dev = queries.shape[0]
    group_rows = resid.shape[0]
    capacity = 2 * rows_dev
    expert_total = req_count * exp_count

    def swap(x):
        return lax.ppermute(x, "head", [(0, 1), (1, 0)])

    early = out_weight.shape[0] * 3 // 8
    attended, first = attend(queries, keys, values, lengths, out_weight, early)
    if exp_count == 4:
        parts = [attended] + [
            lax.ppermute(attended, "exp", [(i, i ^ k) for i in range(exp_count)])
            for k in range(1, exp_count)
        ]
    else:
        parts = [lax.all_gather(attended, "exp", axis=0, tiled=True)]

    staged = stage(
        expert_ids, route_weights, resid, norm_gain[None, :], out_weight, expert_total, capacity, early
    )
    parts, staged = lax.optimization_barrier((parts, staged))
    selector, spread, near_resid, near_gain, second = staged
    keep, give = project(parts, first, second, group_rows)
    hidden, outgoing = dispatch(keep, swap(give), near_resid, selector)
    half = hidden.shape[1]

    def exchange(x):
        return lax.all_to_all(x, ("req", "exp"), split_axis=0, concat_axis=0, tiled=True)

    arrived = exchange(outgoing.reshape(expert_total, capacity, half))
    keep, give = expert(
        arrived, swap(arrived), near_gain, w_gate[0], w_up[0], w_down[0], req_count, exp_count
    )
    returned = exchange(merge(keep, swap(give)))
    mine = combine(spread, returned.reshape(expert_total * capacity, half), hidden)
    return join(mine, swap(mine))


def solution(mesh):
    in_specs = (
        P(("req", "exp"), "head", None),
        P(("req", "exp"), None, "head", None),
        P(("req", "exp"), None, "head", None),
        P(("req", "exp")),
        P("head", "exp"),
        P("req", "exp"),
        P(),
        P("req", None),
        P("req", None),
        P(("req", "exp"), None, "head"),
        P(("req", "exp"), None, "head"),
        P(("req", "exp"), "head", None),
    )
    out_specs = P("req", "exp")
    return jax.shard_map(local, mesh=mesh, in_specs=in_specs, out_specs=out_specs, check_vma=False)
```

```python
import functools
import math

import jax
import jax.numpy as jnp
from jax import lax
from jax.experimental import pallas as pl
from jax.experimental.pallas import tpu as pltpu
from jax.sharding import PartitionSpec as P

F32 = jnp.float32
BF16 = jnp.bfloat16


def whole(memory_space=pltpu.VMEM):
    return pl.BlockSpec(memory_space=memory_space)


def near(x):
    return pltpu.with_memory_space_constraint(x, pltpu.VMEM)


def far(x):
    return pltpu.with_memory_space_constraint(x, pltpu.HBM)


def side(index, span, which):
    return pl.ds(pl.multiple_of((2 * index + which) * span, span), span)


def attend_kernel(
    len_hbm, q_hbm, k_hbm, v_hbm, w_hbm, o_ref, w_ref, len_ref, q_ref, kbuf, vbuf, scr, sems, one,
    *, kv_heads
):
    rows, heads, size = q_ref.shape
    width = kbuf.shape[1]
    per = heads // kv_heads
    tile = 128
    tiles = width // tile
    ask = pltpu.make_async_copy(q_hbm, q_ref, one.at[0])
    span = pltpu.make_async_copy(len_hbm, len_ref, one.at[1])
    load = pltpu.make_async_copy(w_hbm.at[pl.ds(0, w_ref.shape[0])], w_ref, one.at[2])
    kcs = [pltpu.make_async_copy(k_hbm.at[t], kbuf.at[t], sems.at[0, t]) for t in range(rows)]
    vcs = [pltpu.make_async_copy(v_hbm.at[t], vbuf.at[t], sems.at[1, t]) for t in range(rows)]
    for c in [ask, span] + kcs + vcs + [load]:
        c.start()
    lane = lax.broadcasted_iota(jnp.int32, (per, tile), 1)
    group = lane % kv_heads
    slot = lane // kv_heads
    rate = math.log2(math.e) / math.sqrt(size)

    def grouped(fold, unit, reduce):
        res = jnp.zeros((per, tile), F32)
        for g in range(kv_heads):
            one_g = reduce(jnp.where(group == g, fold, unit), axis=1, keepdims=True)
            res = jnp.where(group == g, one_g, res)
        return res

    ask.wait()
    span.wait()
    for c in kcs:
        c.wait()
    weights = []
    for t in range(rows):
        full = lax.dot_general(
            q_ref[t], kbuf[t], (((1,), (1,)), ((), ())), preferred_element_type=F32
        )
        parts = []
        for i in range(tiles):
            cut = slice(i * tile, (i + 1) * tile)
            mine = full[:per, cut]
            for g in range(1, kv_heads):
                mine = jnp.where(group == g, full[g * per : (g + 1) * per, cut], mine)
            live = slot < len_ref[t] - i * (tile // kv_heads)
            parts.append(jnp.where(live, mine, -1e30))
        top = grouped(functools.reduce(jnp.maximum, parts), -1e30, jnp.max)
        raised = [jnp.exp2((p - top) * rate) for p in parts]
        share = 1.0 / grouped(functools.reduce(jnp.add, raised), 0.0, jnp.sum)
        soft = [(r * share).astype(BF16) for r in raised]
        weights.append(
            jnp.concatenate(
                [
                    jnp.concatenate([jnp.where(group == g, w, jnp.zeros_like(w)) for w in soft], axis=1)
                    for g in range(kv_heads)
                ],
                axis=0,
            )
        )
    for c in vcs:
        c.wait()
    for t in range(rows):
        scr[t * heads : (t + 1) * heads, :] = jnp.dot(
            weights[t], vbuf[t], preferred_element_type=F32
        )
    for j in range(heads):
        o_ref[:, j * size : (j + 1) * size] = scr[pl.ds(j, rows, stride=heads), :].astype(BF16)
    load.wait()


def attend(queries, keys, values, lengths, out_weight, early):
    rows, heads, size = queries.shape
    slots, kv_heads = keys.shape[1:3]
    flat = (rows, slots * kv_heads, size)
    return pl.pallas_call(
        functools.partial(attend_kernel, kv_heads=kv_heads),
        out_shape=(
            pltpu.VMEM((rows, heads * size), BF16),
            pltpu.VMEM((early, out_weight.shape[1]), BF16),
        ),
        in_specs=[whole(pltpu.HBM)] * 5,
        out_specs=(whole(), whole()),
        scratch_shapes=[
            pltpu.SMEM((rows,), jnp.int32),
            pltpu.VMEM(queries.shape, BF16),
            pltpu.VMEM(flat, BF16),
            pltpu.VMEM(flat, BF16),
            pltpu.VMEM((rows * heads, size), F32),
            pltpu.SemaphoreType.DMA((2, rows)),
            pltpu.SemaphoreType.DMA((3,)),
        ],
        compiler_params=pltpu.CompilerParams(vmem_limit_bytes=8 * 2**20),
        name="attend",
    )(*map(far, (lengths, queries, keys.reshape(flat), values.reshape(flat), out_weight)))


def stage_kernel(
    ids_hbm, weight_hbm, resid_hbm, gain_hbm, w_hbm,
    sel_ref, spread_ref, resid_ref, gain_ref, w_ref, ids_ref, weight_ref, sems,
    *, capacity,
):
    tail = w_hbm.at[pl.ds(w_hbm.shape[0] - w_ref.shape[0], w_ref.shape[0])]
    pairs = (
        (ids_hbm, ids_ref),
        (weight_hbm, weight_ref),
        (tail, w_ref),
        (resid_hbm, resid_ref),
        (gain_hbm, gain_ref),
    )
    loads = [pltpu.make_async_copy(a, b, sems.at[i]) for i, (a, b) in enumerate(pairs)]
    for c in loads:
        c.start()
    total, rows = sel_ref.shape
    experts = total // capacity
    loads[0].wait()
    loads[1].wait()
    expert = lax.broadcasted_iota(jnp.int32, (experts, rows), 0)
    chosen = jnp.zeros((experts, rows), F32)
    weight = jnp.zeros((experts, rows), F32)
    for k in range(ids_ref.shape[0]):
        hit = ids_ref[k : k + 1, :] == expert
        chosen = jnp.where(hit, 1.0, chosen)
        weight = weight + jnp.where(hit, weight_ref[k : k + 1, :], 0.0)
    before = lax.broadcasted_iota(jnp.int32, (rows, rows), 0)
    after = lax.broadcasted_iota(jnp.int32, (rows, rows), 1)
    upto = jnp.where(before <= after, 1.0, 0.0).astype(BF16)
    place = jnp.dot(chosen.astype(BF16), upto, preferred_element_type=F32) - 1.0
    place = jnp.where(chosen > 0.0, place, -1.0)
    seat = lax.broadcasted_iota(jnp.int32, (experts, capacity, rows), 1).astype(F32)
    taken = jnp.broadcast_to(place[:, None, :], seat.shape) == seat
    shares = jnp.where(taken, jnp.broadcast_to(weight[:, None, :], seat.shape), 0.0)
    sel_ref[...] = jnp.where(taken, 1.0, 0.0).reshape(total, rows).astype(BF16)
    spread_ref[...] = shares.reshape(total, rows).T
    for c in loads[2:]:
        c.wait()


def stage(expert_ids, route_weights, resid, gain, out_weight, experts, capacity, early):
    rows, top = expert_ids.shape
    total = experts * capacity
    depth, width = out_weight.shape
    return pl.pallas_call(
        functools.partial(stage_kernel, capacity=capacity),
        out_shape=(
            pltpu.VMEM((total, rows), BF16),
            pltpu.VMEM((rows, total), F32),
            pltpu.VMEM(resid.shape, BF16),
            pltpu.VMEM(gain.shape, F32),
            pltpu.VMEM((depth - early, width), BF16),
        ),
        in_specs=[whole(pltpu.HBM)] * 5,
        out_specs=(whole(),) * 5,
        scratch_shapes=[
            pltpu.VMEM((top, rows), jnp.int32),
            pltpu.VMEM((top, rows), F32),
            pltpu.SemaphoreType.DMA((5,)),
        ],
        compiler_params=pltpu.CompilerParams(vmem_limit_bytes=8 * 2**20),
        name="stage",
    )(*map(far, (expert_ids.T, route_weights.T, resid, gain, out_weight)))


def project_kernel(*refs, pieces):
    parts = refs[:pieces]
    first_ref, second_ref, x_ref, give_ref = refs[pieces:]
    loaded = [p[...].astype(F32) for p in parts]
    if pieces > 1:
        place = lax.axis_index("exp")
        blocks = []
        for b in range(pieces):
            picked = loaded[0]
            for k in range(1, pieces):
                picked = jnp.where((place ^ k) == b, loaded[k], picked)
            blocks.append(picked)
        x = jnp.concatenate(blocks, axis=0)
    else:
        x = loaded[0]
    x_ref[...] = x.astype(BF16)
    half_product(x_ref, first_ref, second_ref, give_ref, 1 - lax.axis_index("head"))


def half_product(x_ref, first_ref, second_ref, o_ref, which):
    early = first_ref.shape[0]
    cut = side(0, o_ref.shape[1], which)
    o_ref[...] = jnp.dot(x_ref[:, :early], first_ref[:, cut], preferred_element_type=F32) + jnp.dot(
        x_ref[:, early:], second_ref[:, cut], preferred_element_type=F32
    )


def keep_kernel(x_ref, first_ref, second_ref, o_ref):
    half_product(x_ref, first_ref, second_ref, o_ref, lax.axis_index("head"))


def keep_half(x, first, second):
    return pl.pallas_call(
        keep_kernel,
        out_shape=pltpu.VMEM((x.shape[0], first.shape[1] // 2), F32),
        in_specs=[whole()] * 3,
        out_specs=whole(),
        compiler_params=pltpu.CompilerParams(vmem_limit_bytes=8 * 2**20),
        name="keep_half",
    )(near(x), near(first), near(second))


def project(parts, first, second, rows):
    half = first.shape[1] // 2
    depth = first.shape[0] + second.shape[0]
    return pl.pallas_call(
        functools.partial(project_kernel, pieces=len(parts)),
        out_shape=(pltpu.VMEM((rows, depth), BF16), pltpu.VMEM((rows, half), F32)),
        in_specs=[whole()] * (len(parts) + 2),
        out_specs=(whole(), whole()),
        compiler_params=pltpu.CompilerParams(vmem_limit_bytes=8 * 2**20),
        name="project",
    )(*map(near, parts), near(first), near(second))


def dispatch_kernel(own_ref, other_ref, resid_ref, sel_ref, hid_ref, out_ref):
    half = own_ref.shape[1]
    resid = jnp.where(lax.axis_index("head") == 0, resid_ref[:, :half], resid_ref[:, half:])
    hidden = resid.astype(F32) + (own_ref[...] + other_ref[...])
    hid_ref[...] = hidden
    out_ref[...] = jnp.dot(sel_ref[...], hidden.astype(BF16), preferred_element_type=F32).astype(BF16)


def dispatch(own, other, resid, selector):
    rows, half = own.shape
    return pl.pallas_call(
        dispatch_kernel,
        out_shape=(
            pltpu.VMEM((rows, half), F32),
            pltpu.VMEM((selector.shape[0], half), BF16),
        ),
        in_specs=[whole()] * 4,
        out_specs=(whole(), whole()),
        compiler_params=pltpu.CompilerParams(vmem_limit_bytes=8 * 2**20),
        name="dispatch",
    )(near(own), near(other), near(resid), near(selector))


def part_product(x_ref, gain_ref, wg_ref, wu_ref, groups, cols, which):
    half = x_ref.shape[2]
    fold = None
    acc = None
    for e in range(cols):
        at = side(e, half, which)
        x = jnp.concatenate([x_ref[s * cols + e].astype(F32) for s in range(groups)], axis=0)
        for i in range(half // 128):
            cut = x[:, i * 128 : (i + 1) * 128]
            fold = cut * cut if fold is None else fold + cut * cut
        scaled = (x * gain_ref[:, at]).astype(BF16)
        both = jnp.concatenate([wg_ref[at, :], wu_ref[at, :]], axis=1)
        part = jnp.dot(scaled, both, preferred_element_type=F32)
        acc = part if acc is None else acc + part
    return acc, fold


def first_kernel(x_ref, gain_ref, wg_ref, wu_ref, wd_ref, acc_ref, fold_ref, *, groups, cols):
    head = lax.axis_index("head")
    acc_ref[...], fold_ref[...] = part_product(x_ref, gain_ref, wg_ref, wu_ref, groups, cols, head)


def expert_first(own, gain, w_gate, w_up, w_down, groups, cols):
    rows = groups * own.shape[1]
    return pl.pallas_call(
        functools.partial(first_kernel, groups=groups, cols=cols),
        out_shape=(pltpu.VMEM((rows, 2 * w_gate.shape[1]), F32), pltpu.VMEM((rows, 128), F32)),
        in_specs=[whole()] * 5,
        out_specs=(whole(), whole()),
        compiler_params=pltpu.CompilerParams(vmem_limit_bytes=8 * 2**20),
        name="expert_first",
    )(*map(near, (own, gain, w_gate, w_up, w_down)))


def half_down(act_ref, wd_ref, o_ref, groups, cols, which):
    items, half = o_ref.shape[1:]
    for e in range(cols):
        y = jnp.dot(act_ref[...], wd_ref[:, side(e, half, which)], preferred_element_type=F32)
        y = y.astype(o_ref.dtype)
        for s in range(groups):
            o_ref[s * cols + e] = y[s * items : (s + 1) * items, :]


def second_kernel(
    x_ref, acc_ref, fold_ref, gain_ref, wg_ref, wu_ref, wd_ref, act_ref, give_ref, *, groups, cols
):
    depth, hid = wg_ref.shape
    other = 1 - lax.axis_index("head")
    acc, fold = part_product(x_ref, gain_ref, wg_ref, wu_ref, groups, cols, other)
    squares = jnp.sum(fold + fold_ref[...], axis=1, keepdims=True)
    acc = (acc + acc_ref[...]) * lax.rsqrt(squares / depth + 1e-06)
    gate, up = acc[:, :hid], acc[:, hid:]
    act_ref[...] = (gate / (1.0 + jnp.exp(-gate)) * up).astype(BF16)
    half_down(act_ref, wd_ref, give_ref, groups, cols, other)


def expert_second(other, acc, fold, gain, w_gate, w_up, w_down, groups, cols):
    return pl.pallas_call(
        functools.partial(second_kernel, groups=groups, cols=cols),
        out_shape=(
            pltpu.VMEM((acc.shape[0], w_gate.shape[1]), BF16),
            pltpu.VMEM(other.shape, BF16),
        ),
        in_specs=[whole()] * 7,
        out_specs=(whole(), whole()),
        compiler_params=pltpu.CompilerParams(vmem_limit_bytes=8 * 2**20),
        name="expert_second",
    )(*map(near, (other, acc, fold, gain, w_gate, w_up, w_down)))


def third_kernel(act_ref, wd_ref, keep_ref, *, groups, cols):
    half_down(act_ref, wd_ref, keep_ref, groups, cols, lax.axis_index("head"))


def expert_third(activated, w_down, shape, groups, cols):
    return pl.pallas_call(
        functools.partial(third_kernel, groups=groups, cols=cols),
        out_shape=pltpu.VMEM(shape, F32),
        in_specs=[whole()] * 2,
        out_specs=whole(),
        compiler_params=pltpu.CompilerParams(vmem_limit_bytes=8 * 2**20),
        name="expert_third",
    )(near(activated), near(w_down))


def merge_kernel(keep_ref, got_ref, o_ref):
    o_ref[...] = (keep_ref[...] + got_ref[...].astype(F32)).astype(BF16)


def merge(keep, got):
    return pl.pallas_call(
        merge_kernel,
        out_shape=pltpu.VMEM(keep.shape, BF16),
        in_specs=[whole(), whole()],
        out_specs=whole(),
        compiler_params=pltpu.CompilerParams(vmem_limit_bytes=8 * 2**20),
        name="merge",
    )(near(keep), near(got))


def combine_kernel(spread_ref, y_ref, hid_ref, o_ref):
    rows = spread_ref.shape[0]
    spread = spread_ref[...]
    high = spread.astype(BF16)
    rest = spread - high.astype(F32)
    mid = rest.astype(BF16)
    low = (rest - mid.astype(F32)).astype(BF16)
    stacked = jnp.concatenate([high, mid, low], axis=0)
    res = jnp.dot(stacked, y_ref[...], preferred_element_type=F32)
    mixture = res[:rows] + (res[rows : 2 * rows] + res[2 * rows :])
    o_ref[...] = (hid_ref[...] + mixture).astype(BF16)


def combine(spread, returned, hidden):
    return pl.pallas_call(
        combine_kernel,
        out_shape=pltpu.VMEM(hidden.shape, BF16),
        in_specs=[whole()] * 3,
        out_specs=whole(),
        compiler_params=pltpu.CompilerParams(vmem_limit_bytes=8 * 2**20),
        name="combine",
    )(near(spread), near(returned), near(hidden))


def join_kernel(own_ref, other_ref, o_ref):
    half = own_ref.shape[1]
    low = lax.axis_index("head") == 0
    o_ref[:, :half] = jnp.where(low, own_ref[...], other_ref[...])
    o_ref[:, half:] = jnp.where(low, other_ref[...], own_ref[...])


def join(own, other):
    rows, half = own.shape
    return pl.pallas_call(
        join_kernel,
        out_shape=jax.ShapeDtypeStruct((rows, 2 * half), BF16),
        in_specs=[whole(), whole()],
        out_specs=whole(),
        compiler_params=pltpu.CompilerParams(vmem_limit_bytes=8 * 2**20),
        name="join",
    )(near(own), near(other))


def local(
    queries,
    keys,
    values,
    lengths,
    out_weight,
    resid,
    norm_gain,
    expert_ids,
    route_weights,
    w_gate,
    w_up,
    w_down,
):
    req_count = lax.axis_size("req")
    exp_count = lax.axis_size("exp")
    rows_dev = queries.shape[0]
    group_rows = resid.shape[0]
    capacity = 2 * rows_dev
    expert_total = req_count * exp_count

    def swap(x):
        return lax.ppermute(x, "head", [(0, 1), (1, 0)])

    early = out_weight.shape[0] * 3 // 8
    attended, first = attend(queries, keys, values, lengths, out_weight, early)
    if exp_count == 4:
        parts = [attended] + [
            lax.ppermute(attended, "exp", [(i, i ^ k) for i in range(exp_count)])
            for k in range(1, exp_count)
        ]
    else:
        parts = [lax.all_gather(attended, "exp", axis=0, tiled=True)]

    staged = stage(
        expert_ids, route_weights, resid, norm_gain[None, :], out_weight, expert_total, capacity, early
    )
    parts, staged = lax.optimization_barrier((parts, staged))
    selector, spread, near_resid, near_gain, second = staged
    joined, give = project(parts, first, second, group_rows)
    got, keep = lax.optimization_barrier((swap(give), keep_half(joined, first, second)))
    hidden, outgoing = dispatch(keep, got, near_resid, selector)
    half = hidden.shape[1]
    sizes = (req_count, exp_count)

    def exchange(x):
        return lax.all_to_all(x, ("req", "exp"), split_axis=0, concat_axis=0, tiled=True)

    arrived = exchange(outgoing.reshape(expert_total, capacity, half))
    other, begun = lax.optimization_barrier(
        (swap(arrived), expert_first(arrived, near_gain, w_gate[0], w_up[0], w_down[0], *sizes))
    )
    activated, give = expert_second(
        other, *begun, near_gain, w_gate[0], w_up[0], w_down[0], *sizes
    )
    got, keep = lax.optimization_barrier(
        (swap(give), expert_third(activated, w_down[0], give.shape, *sizes))
    )
    returned = exchange(merge(keep, got))
    mine = combine(spread, returned.reshape(expert_total * capacity, half), hidden)
    return join(mine, swap(mine))


def solution(mesh):
    in_specs = (
        P(("req", "exp"), "head", None),
        P(("req", "exp"), None, "head", None),
        P(("req", "exp"), None, "head", None),
        P(("req", "exp")),
        P("head", "exp"),
        P("req", "exp"),
        P(),
        P("req", None),
        P("req", None),
        P(("req", "exp"), None, "head"),
        P(("req", "exp"), None, "head"),
        P(("req", "exp"), "head", None),
    )
    out_specs = P("req", "exp")
    return jax.shard_map(local, mesh=mesh, in_specs=in_specs, out_specs=out_specs, check_vma=False)
```

```python
import functools
import math

import jax
import jax.numpy as jnp
from jax import lax
from jax.experimental import pallas as pl
from jax.experimental.pallas import tpu as pltpu
from jax.sharding import PartitionSpec as P

F32 = jnp.float32
BF16 = jnp.bfloat16


def whole(memory_space=pltpu.VMEM):
    return pl.BlockSpec(memory_space=memory_space)


def near(x):
    return pltpu.with_memory_space_constraint(x, pltpu.VMEM)


def far(x):
    return pltpu.with_memory_space_constraint(x, pltpu.HBM)


def side(index, span, which):
    return pl.ds(pl.multiple_of((2 * index + which) * span, span), span)


def attend_kernel(
    len_hbm, q_hbm, k_hbm, v_hbm, o_ref, len_ref, q_ref, kbuf, vbuf, scr, sems, one, *, kv_heads
):
    rows, heads, size = q_ref.shape
    width = kbuf.shape[1]
    per = heads // kv_heads
    tile = 128
    tiles = width // tile
    ask = pltpu.make_async_copy(q_hbm, q_ref, one.at[0])
    span = pltpu.make_async_copy(len_hbm, len_ref, one.at[1])
    kcs = [pltpu.make_async_copy(k_hbm, kbuf, sems.at[0, 0])]
    vcs = [pltpu.make_async_copy(v_hbm, vbuf, sems.at[1, 0])]
    for c in [ask, span] + kcs + vcs:
        c.start()
    lane = lax.broadcasted_iota(jnp.int32, (per, tile), 1)
    group = lane % kv_heads
    slot = lane // kv_heads
    rate = math.log2(math.e) / math.sqrt(size)

    def grouped(fold, unit, reduce):
        res = jnp.zeros((per, tile), F32)
        for g in range(kv_heads):
            one_g = reduce(jnp.where(group == g, fold, unit), axis=1, keepdims=True)
            res = jnp.where(group == g, one_g, res)
        return res

    ask.wait()
    span.wait()
    for c in kcs:
        c.wait()
    weights = []
    for t in range(rows):
        full = lax.dot_general(
            q_ref[t], kbuf[t], (((1,), (1,)), ((), ())), preferred_element_type=F32
        )
        parts = []
        for i in range(tiles):
            cut = slice(i * tile, (i + 1) * tile)
            mine = full[:per, cut]
            for g in range(1, kv_heads):
                mine = jnp.where(group == g, full[g * per : (g + 1) * per, cut], mine)
            live = slot < len_ref[t] - i * (tile // kv_heads)
            parts.append(jnp.where(live, mine, -1e30))
        top = grouped(functools.reduce(jnp.maximum, parts), -1e30, jnp.max)
        raised = [jnp.exp2((p - top) * rate) for p in parts]
        share = 1.0 / grouped(functools.reduce(jnp.add, raised), 0.0, jnp.sum)
        soft = [(r * share).astype(BF16) for r in raised]
        weights.append(
            jnp.concatenate(
                [
                    jnp.concatenate([jnp.where(group == g, w, jnp.zeros_like(w)) for w in soft], axis=1)
                    for g in range(kv_heads)
                ],
                axis=0,
            )
        )
    for c in vcs:
        c.wait()
    for t in range(rows):
        scr[t * heads : (t + 1) * heads, :] = jnp.dot(
            weights[t], vbuf[t], preferred_element_type=F32
        )
    for j in range(heads):
        o_ref[:, j * size : (j + 1) * size] = scr[pl.ds(j, rows, stride=heads), :].astype(BF16)


def attend(queries, keys, values, lengths):
    rows, heads, size = queries.shape
    slots, kv_heads = keys.shape[1:3]
    flat = (rows, slots * kv_heads, size)
    return pl.pallas_call(
        functools.partial(attend_kernel, kv_heads=kv_heads),
        out_shape=pltpu.VMEM((rows, heads * size), BF16),
        in_specs=[whole(pltpu.HBM)] * 4,
        out_specs=whole(),
        scratch_shapes=[
            pltpu.SMEM((rows,), jnp.int32),
            pltpu.VMEM(queries.shape, BF16),
            pltpu.VMEM(flat, BF16),
            pltpu.VMEM(flat, BF16),
            pltpu.VMEM((rows * heads, size), F32),
            pltpu.SemaphoreType.DMA((2, rows)),
            pltpu.SemaphoreType.DMA((2,)),
        ],
        compiler_params=pltpu.CompilerParams(vmem_limit_bytes=8 * 2**20),
        name="attend",
    )(*map(far, (lengths, queries, keys.reshape(flat), values.reshape(flat))))


def stage_kernel(ids_ref, weight_ref, sel_ref, spread_ref, *, capacity):
    total, rows = sel_ref.shape
    experts = total // capacity
    expert = lax.broadcasted_iota(jnp.int32, (experts, rows), 0)
    chosen = jnp.zeros((experts, rows), F32)
    weight = jnp.zeros((experts, rows), F32)
    for k in range(ids_ref.shape[0]):
        hit = ids_ref[k : k + 1, :] == expert
        chosen = jnp.where(hit, 1.0, chosen)
        weight = weight + jnp.where(hit, weight_ref[k : k + 1, :], 0.0)
    before = lax.broadcasted_iota(jnp.int32, (rows, rows), 0)
    after = lax.broadcasted_iota(jnp.int32, (rows, rows), 1)
    upto = jnp.where(before <= after, 1.0, 0.0).astype(BF16)
    place = jnp.dot(chosen.astype(BF16), upto, preferred_element_type=F32) - 1.0
    place = jnp.where(chosen > 0.0, place, -1.0)
    seat = lax.broadcasted_iota(jnp.int32, (experts, capacity, rows), 1).astype(F32)
    taken = jnp.broadcast_to(place[:, None, :], seat.shape) == seat
    shares = jnp.where(taken, jnp.broadcast_to(weight[:, None, :], seat.shape), 0.0)
    sel_ref[...] = jnp.where(taken, 1.0, 0.0).reshape(total, rows).astype(BF16)
    spread_ref[...] = shares.reshape(total, rows).T


def stage(expert_ids, route_weights, experts, capacity):
    rows = expert_ids.shape[0]
    total = experts * capacity
    return pl.pallas_call(
        functools.partial(stage_kernel, capacity=capacity),
        out_shape=(pltpu.VMEM((total, rows), BF16), pltpu.VMEM((rows, total), F32)),
        in_specs=[whole(), whole()],
        out_specs=(whole(), whole()),
        compiler_params=pltpu.CompilerParams(vmem_limit_bytes=8 * 2**20),
        name="stage",
    )(near(expert_ids.T), near(route_weights.T))


def project_kernel(*refs, pieces):
    parts = refs[:pieces]
    w_ref, tail_ref, x_ref, give_ref = refs[pieces:]
    loaded = [p[...].astype(F32) for p in parts]
    if pieces > 1:
        place = lax.axis_index("exp")
        blocks = []
        for b in range(pieces):
            picked = loaded[0]
            for k in range(1, pieces):
                picked = jnp.where((place ^ k) == b, loaded[k], picked)
            blocks.append(picked)
        x = jnp.concatenate(blocks, axis=0)
    else:
        x = loaded[0]
    x_ref[...] = x.astype(BF16)
    half_product(x_ref, w_ref, tail_ref, give_ref, 1 - lax.axis_index("head"))


def half_product(x_ref, w_ref, tail_ref, o_ref, which):
    cut = side(0, o_ref.shape[1], which)
    early = w_ref.shape[0] - tail_ref.shape[0]
    o_ref[...] = jnp.dot(
        x_ref[:, :early], w_ref[:early, cut], preferred_element_type=F32
    ) + jnp.dot(x_ref[:, early:], tail_ref[:, cut], preferred_element_type=F32)


def keep_kernel(x_ref, w_ref, tail_ref, o_ref):
    half_product(x_ref, w_ref, tail_ref, o_ref, lax.axis_index("head"))


def keep_half(x, out_weight, tail):
    return pl.pallas_call(
        keep_kernel,
        out_shape=pltpu.VMEM((x.shape[0], out_weight.shape[1] // 2), F32),
        in_specs=[whole()] * 3,
        out_specs=whole(),
        compiler_params=pltpu.CompilerParams(vmem_limit_bytes=8 * 2**20),
        name="keep_half",
    )(near(x), near(out_weight), near(tail))


def project(parts, out_weight, tail, rows):
    depth, width = out_weight.shape
    return pl.pallas_call(
        functools.partial(project_kernel, pieces=len(parts)),
        out_shape=(pltpu.VMEM((rows, depth), BF16), pltpu.VMEM((rows, width // 2), F32)),
        in_specs=[whole()] * (len(parts) + 2),
        out_specs=(whole(), whole()),
        compiler_params=pltpu.CompilerParams(vmem_limit_bytes=8 * 2**20),
        name="project",
    )(*map(near, parts), near(out_weight), near(tail))


def dispatch_kernel(own_ref, other_ref, resid_ref, sel_ref, hid_ref, out_ref):
    half = own_ref.shape[1]
    resid = jnp.where(lax.axis_index("head") == 0, resid_ref[:, :half], resid_ref[:, half:])
    hidden = resid.astype(F32) + (own_ref[...] + other_ref[...])
    hid_ref[...] = hidden
    out_ref[...] = jnp.dot(sel_ref[...], hidden.astype(BF16), preferred_element_type=F32).astype(BF16)


def dispatch(own, other, resid, selector):
    rows, half = own.shape
    return pl.pallas_call(
        dispatch_kernel,
        out_shape=(
            pltpu.VMEM((rows, half), F32),
            pltpu.VMEM((selector.shape[0], half), BF16),
        ),
        in_specs=[whole()] * 4,
        out_specs=(whole(), whole()),
        compiler_params=pltpu.CompilerParams(vmem_limit_bytes=8 * 2**20),
        name="dispatch",
    )(near(own), near(other), near(resid), near(selector))


def part_product(x_ref, gain_ref, wg_ref, wu_ref, groups, cols, which):
    half = x_ref.shape[2]
    fold = None
    acc = None
    for e in range(cols):
        at = side(e, half, which)
        x = jnp.concatenate([x_ref[s * cols + e].astype(F32) for s in range(groups)], axis=0)
        for i in range(half // 128):
            cut = x[:, i * 128 : (i + 1) * 128]
            fold = cut * cut if fold is None else fold + cut * cut
        scaled = (x * gain_ref[:, at]).astype(BF16)
        both = jnp.concatenate([wg_ref[at, :], wu_ref[at, :]], axis=1)
        part = jnp.dot(scaled, both, preferred_element_type=F32)
        acc = part if acc is None else acc + part
    return acc, fold


def first_kernel(x_ref, gain_ref, wg_ref, wu_ref, wd_ref, acc_ref, fold_ref, *, groups, cols):
    head = lax.axis_index("head")
    acc_ref[...], fold_ref[...] = part_product(x_ref, gain_ref, wg_ref, wu_ref, groups, cols, head)


def expert_first(own, gain, w_gate, w_up, w_down, groups, cols):
    rows = groups * own.shape[1]
    return pl.pallas_call(
        functools.partial(first_kernel, groups=groups, cols=cols),
        out_shape=(pltpu.VMEM((rows, 2 * w_gate.shape[1]), F32), pltpu.VMEM((rows, 128), F32)),
        in_specs=[whole()] * 5,
        out_specs=(whole(), whole()),
        compiler_params=pltpu.CompilerParams(vmem_limit_bytes=8 * 2**20),
        name="expert_first",
    )(*map(near, (own, gain, w_gate, w_up, w_down)))


def half_down(act_ref, wd_ref, o_ref, groups, cols, which):
    items, half = o_ref.shape[1:]
    for e in range(cols):
        y = jnp.dot(act_ref[...], wd_ref[:, side(e, half, which)], preferred_element_type=F32)
        y = y.astype(o_ref.dtype)
        for s in range(groups):
            o_ref[s * cols + e] = y[s * items : (s + 1) * items, :]


def second_kernel(
    x_ref, acc_ref, fold_ref, gain_ref, wg_ref, wu_ref, wd_ref, act_ref, give_ref, *, groups, cols
):
    depth, hid = wg_ref.shape
    other = 1 - lax.axis_index("head")
    acc, fold = part_product(x_ref, gain_ref, wg_ref, wu_ref, groups, cols, other)
    squares = jnp.sum(fold + fold_ref[...], axis=1, keepdims=True)
    acc = (acc + acc_ref[...]) * lax.rsqrt(squares / depth + 1e-06)
    gate, up = acc[:, :hid], acc[:, hid:]
    act_ref[...] = (gate / (1.0 + jnp.exp(-gate)) * up).astype(BF16)
    half_down(act_ref, wd_ref, give_ref, groups, cols, other)


def expert_second(other, acc, fold, gain, w_gate, w_up, w_down, groups, cols):
    return pl.pallas_call(
        functools.partial(second_kernel, groups=groups, cols=cols),
        out_shape=(
            pltpu.VMEM((acc.shape[0], w_gate.shape[1]), BF16),
            pltpu.VMEM(other.shape, BF16),
        ),
        in_specs=[whole()] * 7,
        out_specs=(whole(), whole()),
        compiler_params=pltpu.CompilerParams(vmem_limit_bytes=8 * 2**20),
        name="expert_second",
    )(*map(near, (other, acc, fold, gain, w_gate, w_up, w_down)))


def third_kernel(act_ref, wd_ref, keep_ref, *, groups, cols):
    half_down(act_ref, wd_ref, keep_ref, groups, cols, lax.axis_index("head"))


def expert_third(activated, w_down, shape, groups, cols):
    return pl.pallas_call(
        functools.partial(third_kernel, groups=groups, cols=cols),
        out_shape=pltpu.VMEM(shape, F32),
        in_specs=[whole()] * 2,
        out_specs=whole(),
        compiler_params=pltpu.CompilerParams(vmem_limit_bytes=8 * 2**20),
        name="expert_third",
    )(near(activated), near(w_down))


def merge_kernel(keep_ref, got_ref, o_ref):
    o_ref[...] = (keep_ref[...] + got_ref[...].astype(F32)).astype(BF16)


def merge(keep, got):
    return pl.pallas_call(
        merge_kernel,
        out_shape=pltpu.VMEM(keep.shape, BF16),
        in_specs=[whole(), whole()],
        out_specs=whole(),
        compiler_params=pltpu.CompilerParams(vmem_limit_bytes=8 * 2**20),
        name="merge",
    )(near(keep), near(got))


def combine_kernel(spread_ref, y_ref, hid_ref, o_ref):
    rows = spread_ref.shape[0]
    spread = spread_ref[...]
    high = spread.astype(BF16)
    rest = spread - high.astype(F32)
    mid = rest.astype(BF16)
    low = (rest - mid.astype(F32)).astype(BF16)
    stacked = jnp.concatenate([high, mid, low], axis=0)
    res = jnp.dot(stacked, y_ref[...], preferred_element_type=F32)
    mixture = res[:rows] + (res[rows : 2 * rows] + res[2 * rows :])
    o_ref[...] = (hid_ref[...] + mixture).astype(BF16)


def combine(spread, returned, hidden):
    return pl.pallas_call(
        combine_kernel,
        out_shape=pltpu.VMEM(hidden.shape, BF16),
        in_specs=[whole()] * 3,
        out_specs=whole(),
        compiler_params=pltpu.CompilerParams(vmem_limit_bytes=8 * 2**20),
        name="combine",
    )(near(spread), near(returned), near(hidden))


def join_kernel(own_ref, other_ref, o_ref):
    half = own_ref.shape[1]
    low = lax.axis_index("head") == 0
    o_ref[:, :half] = jnp.where(low, own_ref[...], other_ref[...])
    o_ref[:, half:] = jnp.where(low, other_ref[...], own_ref[...])


def join(own, other):
    rows, half = own.shape
    return pl.pallas_call(
        join_kernel,
        out_shape=jax.ShapeDtypeStruct((rows, 2 * half), BF16),
        in_specs=[whole(), whole()],
        out_specs=whole(),
        compiler_params=pltpu.CompilerParams(vmem_limit_bytes=8 * 2**20),
        name="join",
    )(near(own), near(other))


def local(
    queries,
    keys,
    values,
    lengths,
    out_weight,
    resid,
    norm_gain,
    expert_ids,
    route_weights,
    w_gate,
    w_up,
    w_down,
):
    req_count = lax.axis_size("req")
    exp_count = lax.axis_size("exp")
    rows_dev = queries.shape[0]
    group_rows = resid.shape[0]
    capacity = 2 * rows_dev
    expert_total = req_count * exp_count

    def swap(x):
        return lax.ppermute(x, "head", [(0, 1), (1, 0)])

    attended = attend(queries, keys, values, lengths)
    if exp_count == 4:
        parts = [attended] + [
            lax.ppermute(attended, "exp", [(i, i ^ k) for i in range(exp_count)])
            for k in range(1, exp_count)
        ]
    else:
        parts = [lax.all_gather(attended, "exp", axis=0, tiled=True)]

    selector, spread = stage(expert_ids, route_weights, expert_total, capacity)
    parts, selector, spread = lax.optimization_barrier((parts, selector, spread))
    tail = out_weight[out_weight.shape[0] * 5 // 8 :]
    near_resid, near_gain = resid, norm_gain[None, :]
    joined, give = project(parts, out_weight, tail, group_rows)
    got, keep = lax.optimization_barrier((swap(give), keep_half(joined, out_weight, tail)))
    hidden, outgoing = dispatch(keep, got, near_resid, selector)
    half = hidden.shape[1]
    sizes = (req_count, exp_count)

    def exchange(x):
        return lax.all_to_all(x, ("req", "exp"), split_axis=0, concat_axis=0, tiled=True)

    arrived = exchange(outgoing.reshape(expert_total, capacity, half))
    other, begun = lax.optimization_barrier(
        (swap(arrived), expert_first(arrived, near_gain, w_gate[0], w_up[0], w_down[0], *sizes))
    )
    activated, give = expert_second(
        other, *begun, near_gain, w_gate[0], w_up[0], w_down[0], *sizes
    )
    got, keep = lax.optimization_barrier(
        (swap(give), expert_third(activated, w_down[0], give.shape, *sizes))
    )
    returned = exchange(merge(keep, got))
    mine = combine(spread, returned.reshape(expert_total * capacity, half), hidden)
    return join(mine, swap(mine))


def solution(mesh):
    in_specs = (
        P(("req", "exp"), "head", None),
        P(("req", "exp"), None, "head", None),
        P(("req", "exp"), None, "head", None),
        P(("req", "exp")),
        P("head", "exp"),
        P("req", "exp"),
        P(),
        P("req", None),
        P("req", None),
        P(("req", "exp"), None, "head"),
        P(("req", "exp"), None, "head"),
        P(("req", "exp"), "head", None),
    )
    out_specs = P("req", "exp")
    return jax.shard_map(local, mesh=mesh, in_specs=in_specs, out_specs=out_specs, check_vma=False)
```
